32 devices in a mesh: rows: 8 (over z, y), cols: 4 (over x, core).
Axes of the slice: x: 2, y: 2, z: 4, core: 2. Of those that a mesh axis runs over, the one named last changes fastest.
Arguments:
- factor: bfloat16 [4096, 256], P(('rows', 'cols')), may hold values from -0.09375 to 0.09375
- cores: bfloat16 [4, 256, 256], replicated, as said below
- tile_values: bfloat16 [4, 96, 512, 128], P(None, 'rows', 'cols'), may hold values from -56 to 56
- tile_rows: int32 [4, 8, 48], P(None, 'rows', 'cols'), may hold values from 0 to 3
- tile_cols: int32 [4, 8, 48], P(None, 'rows', 'cols'), may hold values from 0 to 7
- tile_counts: int32 [4, 8, 4], P(None, 'rows', 'cols'), may hold values from 3 to 12, as said below
Outputs:
- factor_new: bfloat16 [4096, 256], P(('rows', 'cols'))
- cores_new: float32 [4, 256, 256], replicated
The draws below stay inside these ranges and needn't reach their ends.
Inputs may be any that keep to these rules, and one draw needn't show every extreme that they name: cores are dominated by their positive diagonals. `tile_counts`: every relation has some device whose 12 slots are all used. `tile_rows`: several slots may name the same tile.
All inputs are finite; a program needn't handle non-finite values.
Results may differ from the reference program's by a relative error of at most 0.0034.
The reference program's roundings to bfloat16 on the way count: a program that leaves them out, or rounds other values in their place, can miss the bound.
Values may be sent and summed in bfloat16 or wider, within the bound.
No kernel may reach another device: no remote copies, remote signals or barrier semaphores. Data moves between devices by JAX's collectives and lax.ppermute only.
A program may use at most 128 MiB of HBM per device.

```python
import math
import jax
import jax.numpy as jnp
import numpy as np
from jax import lax

R = 256
TILE = 128
K = 4
EDEV = 128
SLOTS = 12
NE = 4096
PANEL = 512
PTR = 4
CTB = 8
N_ROWS = 8
N_COLS = 4


def draw_cores(key, part):
    key_diag = jax.random.fold_in(key, 11)
    key_spread = jax.random.fold_in(key, 12)
    diagonal = 0.6 + 0.8 * jax.random.uniform(key_diag, (K, R), jnp.float32)
    spread_part = jax.random.normal(key_spread, (K, R, R), jnp.float32) * (0.6 / math.sqrt(R))
    identity = jnp.eye(R, dtype=jnp.float32)[None, :, :]
    return (spread_part * (1.0 - identity) + diagonal[:, :, None] * identity).astype(jnp.bfloat16)


def draw_tile_counts(key, part):
    key_counts = jax.random.fold_in(key, 21)
    key_chosen = jax.random.fold_in(key, 22)
    lowest = max(1, SLOTS // 4)
    counts = jax.random.randint(key_counts, (K, N_ROWS, N_COLS), lowest, SLOTS + 1, jnp.int32)
    chosen = jax.random.randint(key_chosen, (K,), 0, N_ROWS * N_COLS, jnp.int32)
    flattened_index = jnp.arange(N_ROWS * N_COLS, dtype=jnp.int32).reshape(1, N_ROWS, N_COLS)
    return jnp.where(flattened_index == chosen[:, None, None], SLOTS, counts).astype(jnp.int32)


def plant(result, rng, smallest, largest):
    shape = result.shape
    place = [jax.random.randint(jax.random.fold_in(rng, axis), (), 0, shape[axis]) for axis in range(len(shape))]
    result = result.at[tuple(place)].set(smallest)
    longest = shape.index(max(shape))
    place[longest] = (place[longest] + 1) % shape[longest]
    return result.at[tuple(place)].set(largest)


def level_of(rng, shape, split, smallest, largest):
    gain = 1.0
    for dim, blocks in split:
        steps = jax.random.uniform(jax.random.fold_in(jax.random.fold_in(rng, 6), dim), (blocks,), jnp.float32, smallest / len(split), largest / len(split))
        gain = gain * jnp.repeat(jnp.exp(steps), shape[dim] // blocks).reshape((-1,) + (1,) * (len(shape) - 1 - dim))
    return gain


def rank_table(number_of, skew):
    weights = [(1 << 20) // math.isqrt(standing ** skew) + 1 for standing in range(1, number_of + 1)]
    spread = 1 + sum(weights) // (1 << 30)
    return np.cumsum(np.array([max(1, weight // spread) for weight in weights]))


def ranked_ids(rng, dims, amount, slope):
    table = rank_table(amount, slope)
    ticket = jax.random.randint(jax.random.fold_in(rng, 1), dims, 0, int(table[amount - 1]))
    grade = jnp.searchsorted(jnp.asarray(table, jnp.int32), ticket, side="right")
    return jax.random.permutation(jax.random.fold_in(rng, 2), amount)[grade].astype(jnp.int32)


def bell_draw(own_key, extent, scale, most, cuts=(), held_as=jnp.bfloat16):
    entries = scale * jax.random.normal(own_key, extent, jnp.float32)
    if cuts:
        entries = entries * level_of(own_key, extent, cuts, -0.22, 0.18)
    return jnp.clip(entries, -most, most).astype(held_as)


def setup_inputs(seed: int = 0) -> dict:
    key_of = jax.random.split(jax.random.key(seed), 7)
    return {
        "factor": bell_draw(key_of[0], (NE, R), NE ** -0.5, 0.09375, ((0, 32),)),
        "cores": draw_cores(jax.random.fold_in(key_of[6], 71), 0),
        "tile_values": bell_draw(key_of[2], (K, N_ROWS * SLOTS, N_COLS * TILE, TILE), (4 * K * (NE * PTR / (2 * K * TILE * N_COLS * SLOTS)) ** 0.5), 56.0, ((1, 8), (2, 4))),
        "tile_rows": plant(ranked_ids(key_of[3], (K, N_ROWS, N_COLS * SLOTS), PTR, 2), jax.random.fold_in(key_of[3], 3), 0, PTR - 1).astype(jnp.int32),
        "tile_cols": plant(jax.random.randint(key_of[4], (K, N_ROWS, N_COLS * SLOTS), 0, CTB), jax.random.fold_in(key_of[4], 1), 0, CTB - 1).astype(jnp.int32),
        "tile_counts": draw_tile_counts(jax.random.fold_in(key_of[6], 71), 0),
    }


ridge_weight = 0.1

def normal_system(summed_gram_matrix, cores_float32):
    direct_part = jnp.einsum('krs,st,kqt->rq', cores_float32, summed_gram_matrix, cores_float32, precision=lax.Precision.HIGHEST)
    reflected_part = jnp.einsum('euh,uc,eca->ha', cores_float32, summed_gram_matrix, cores_float32, precision=lax.Precision.HIGHEST)
    return direct_part + reflected_part + ridge_weight * jnp.eye(summed_gram_matrix.shape[0], dtype=jnp.float32)

def solve_rows(cholesky_lhs, numerator):
    halfway = lax.linalg.triangular_solve(cholesky_lhs, numerator.T, left_side=True, lower=True)
    return lax.linalg.triangular_solve(cholesky_lhs, halfway, left_side=True, lower=True, transpose_a=True).T

def whiten(cholesky_new, core_num):
    relations, rank_size, _ = core_num.shape
    stacked = core_num.transpose(1, 0, 2).reshape(rank_size, relations * rank_size)
    halfway = lax.linalg.triangular_solve(cholesky_new, stacked, left_side=True, lower=True)
    flipped = halfway.reshape(rank_size, relations, rank_size).transpose(2, 1, 0).reshape(rank_size, relations * rank_size)
    second = lax.linalg.triangular_solve(cholesky_new, flipped, left_side=True, lower=True)
    return second.reshape(rank_size, relations, rank_size).transpose(1, 2, 0)

def reference(factor, cores, tile_values, tile_rows, tile_cols, tile_counts):
    cores_float32 = cores.astype(jnp.float32)
    gram_old = jnp.dot(factor.T.astype(jnp.float32), factor.astype(jnp.float32), preferred_element_type=jnp.float32)
    cholesky_lhs = jnp.linalg.cholesky(normal_system(gram_old, cores_float32))
    rotated = jnp.einsum('er,krs->kes', factor.astype(jnp.float32), cores_float32).astype(jnp.bfloat16)
    factor_tiles = factor.reshape(NE // TILE, TILE, R)
    rotated_tiles = rotated.reshape(K, NE // TILE, TILE, R)
    all_values = tile_values.reshape(K, N_ROWS, SLOTS, N_COLS, TILE, TILE).transpose(1, 0, 3, 2, 4, 5)
    all_rows = tile_rows.reshape(K, N_ROWS, N_COLS, SLOTS).transpose(1, 0, 2, 3)
    all_cols = tile_cols.reshape(K, N_ROWS, N_COLS, SLOTS).transpose(1, 0, 2, 3)
    all_counts = tile_counts.transpose(1, 0, 2)
    panel_ids = jnp.arange(N_ROWS, dtype=jnp.int32)
    relation_ids = jnp.arange(K, dtype=jnp.int32)[:, None, None]
    device_cols = jnp.arange(N_COLS, dtype=jnp.int32)[None, :, None]

    def placement(panel_rows, panel_cols, panel_entry_counts, panel_id):
        live_mask = (jnp.arange(SLOTS, dtype=jnp.int32)[None, None, :] < panel_entry_counts[:, :, None]).astype(jnp.float32)
        global_rows = panel_id * PTR + panel_rows
        global_cols = (panel_cols * TILE // EDEV * PANEL + device_cols * EDEV + panel_cols * TILE % EDEV) // TILE
        return (live_mask, global_rows.astype(jnp.int32), global_cols.astype(jnp.int32))

    def first_pass(column_sum, panel_input_tiles):
        panel_values, panel_rows, panel_cols, panel_entry_counts, panel_id = panel_input_tiles
        live_mask, global_rows, global_cols = placement(panel_rows, panel_cols, panel_entry_counts, panel_id)
        values32 = panel_values.astype(jnp.float32)
        picked = factor_tiles[global_cols].astype(jnp.float32)
        products = jnp.einsum('kcsij,kcsjr->kcsir', values32, picked) * live_mask[..., None, None]
        onehot = (panel_rows[..., None] == jnp.arange(PTR, dtype=jnp.int32)).astype(jnp.float32)
        row_block = jnp.einsum('kcst,kcsir->ktir', onehot, products, precision=lax.Precision.HIGHEST)
        rotated_selection = rotated_tiles[relation_ids, global_rows].astype(jnp.float32)
        back_products = jnp.einsum('kcsij,kcsir->kcsjr', values32, rotated_selection) * live_mask[..., None, None]
        column_sum = column_sum.at[global_cols].add(back_products)
        return (column_sum, row_block)
    column_start = jnp.zeros((NE // TILE, TILE, R), jnp.float32)
    column_sum, row_blocks = lax.scan(first_pass, column_start, (all_values, all_rows, all_cols, all_counts, panel_ids))
    direct = row_blocks.transpose(1, 0, 2, 3, 4).reshape(K, NE, R)
    numerator = jnp.einsum('kes,kqs->eq', direct, cores_float32, precision=lax.Precision.HIGHEST) + column_sum.reshape(NE, R)
    factor_new = solve_rows(cholesky_lhs, numerator).astype(jnp.bfloat16)
    new_tiles = factor_new.reshape(NE // TILE, TILE, R)

    def second_pass(core_sum, panel_input_tiles):
        panel_values, panel_rows, panel_cols, panel_entry_counts, panel_id = panel_input_tiles
        live_mask, global_rows, global_cols = placement(panel_rows, panel_cols, panel_entry_counts, panel_id)
        values32 = panel_values.astype(jnp.float32)
        upper = jnp.einsum('kcsij,kcsir->kcsjr', values32, new_tiles[global_rows].astype(jnp.float32)).astype(jnp.bfloat16)
        upper = jnp.where(live_mask[..., None, None] > 0, upper, jnp.zeros_like(upper))
        core_sum = core_sum + jnp.einsum('kcsjr,kcsjq->krq', upper.astype(jnp.float32), new_tiles[global_cols].astype(jnp.float32))
        return (core_sum, None)
    core_num, _ = lax.scan(second_pass, jnp.zeros((K, R, R), jnp.float32), (all_values, all_rows, all_cols, all_counts, panel_ids))
    gram_new = jnp.dot(factor_new.T.astype(jnp.float32), factor_new.astype(jnp.float32), preferred_element_type=jnp.float32)
    cores_new = whiten(jnp.linalg.cholesky(gram_new), core_num)
    return (factor_new, cores_new)
```

```python
import functools

import jax
import jax.numpy as jnp
from jax import lax
from jax.experimental import pallas as pl
from jax.experimental.pallas import tpu as pltpu
from jax.sharding import PartitionSpec as P

ridge_weight = 0.1
value_bound = 160.0
product_bound = 672.0
f16_top = 30000.0


def params():
    return pltpu.CompilerParams(vmem_limit_bytes=48 * 1024 * 1024)


def swap(x, axis, mask):
    size = lax.axis_size(axis)
    return lax.ppermute(x, axis, [(i, i ^ mask) for i in range(size)])


def bits_of(axis):
    return lax.axis_size(axis).bit_length() - 1


def reversed_slot(slot, bits):
    out = 0
    for b in range(bits):
        out = out + (((slot >> b) & 1) << (bits - 1 - b))
    return out


def gather_cols(x):
    for b in range(bits_of("cols")):
        x = jnp.concatenate([x, swap(x, "cols", 1 << b)], axis=0)
    return x


def gather_rows(x):
    half = lax.axis_size("rows") // 2
    even = jnp.concatenate([x] + [swap(x, "rows", 2 * i) for i in range(1, half)], axis=0)
    odd = swap(even, "rows", 1)
    return jnp.concatenate([even, odd], axis=0)


def tree_sum(parts):
    while len(parts) > 1:
        parts = [parts[i] + parts[i + 1] for i in range(0, len(parts), 2)]
    return parts[0]


def half_of(x, scale):
    return (x * scale).astype(jnp.float16)


def scatter_cols(x, scale):
    for b in range(bits_of("cols")):
        keep, give = jnp.split(x, 2, axis=0)
        if b == 0:
            x = keep + swap(give, "cols", 1)
        else:
            x = keep + swap(half_of(give, scale), "cols", 1 << b).astype(jnp.float32) / scale
    return x


def dot(a, b, dims=((1,), (0,)), precision=None):
    return lax.dot_general(
        a, b, (dims, ((), ())), preferred_element_type=jnp.float32, precision=precision
    )


def first_kernel(rows_ref, cols_ref, counts_ref, tiles_ref, factors_ref, panel_ref, cores_ref,
                 direct_ref, back_ref, acc_ref, turned_ref, sums_ref, *, bits_c, half):
    relations, slots = tiles_ref.shape[0], tiles_ref.shape[1]
    tile = tiles_ref.shape[2]
    panels = panel_ref.shape[0] // tile
    my_row = lax.axis_index("rows")
    my_col = lax.axis_index("cols")
    sums_ref[...] = jnp.zeros_like(sums_ref)
    for k in range(relations):
        core = cores_ref[k]
        for i in range(panels):
            rotated = dot(panel_ref[i * tile:(i + 1) * tile, :], core).astype(jnp.bfloat16)
            turned_ref[i] = rotated.T
        acc_ref[...] = jnp.zeros_like(acc_ref)
        for s in range(slots):
            live = s < counts_ref[k, 0, 0]
            values = tiles_ref[k, s]
            values = jnp.where(live, values, jnp.zeros_like(values))
            col = cols_ref[k, 0, s] ^ my_row
            col = (col & 1) * half + (col >> 1)
            row = rows_ref[k, 0, s] ^ my_col
            acc_ref[row] += dot(values, factors_ref[col])
            sums_ref[col] += dot(turned_ref[row], values)
        for i in range(panels):
            whole = acc_ref[i]
            high = whole.astype(jnp.bfloat16)
            low = (whole - high.astype(jnp.float32)).astype(jnp.bfloat16)
            part = dot(high, core, ((1,), (1,))) + dot(low, core, ((1,), (1,)))
            place = reversed_slot(i, bits_c)
            if k == 0:
                direct_ref[place] = part
            else:
                direct_ref[place] += part
    for g in range(sums_ref.shape[0]):
        back_ref[g] = sums_ref[g].T


def first_pass(rows, cols, counts, tiles, factors, panel, cores):
    relations, slots, tile, _ = tiles.shape
    rank = cores.shape[-1]
    n_rows, n_cols = lax.axis_size("rows"), lax.axis_size("cols")
    smem = pl.BlockSpec(memory_space=pltpu.SMEM)
    vmem = pl.BlockSpec(memory_space=pltpu.VMEM)
    return pl.pallas_call(
        functools.partial(first_kernel, bits_c=bits_of("cols"), half=n_rows // 2),
        out_shape=(
            jax.ShapeDtypeStruct((n_cols, tile, rank), jnp.float32),
            jax.ShapeDtypeStruct((n_rows, tile, rank), jnp.float32),
        ),
        in_specs=[smem, smem, smem, vmem, vmem, vmem, vmem],
        out_specs=(vmem, vmem),
        scratch_shapes=[
            pltpu.VMEM((n_cols, tile, rank), jnp.float32),
            pltpu.VMEM((n_cols, rank, tile), jnp.bfloat16),
            pltpu.VMEM((n_rows, rank, tile), jnp.float32),
        ],
        compiler_params=params(),
        name="first_pass",
    )(rows, cols, counts, tiles, factors.reshape(n_rows, tile, rank), panel, cores)


def second_kernel(rows_ref, cols_ref, counts_ref, tiles_ref, factors_ref, panel_ref,
                  out_ref, turned_ref, upper_ref, picked_ref, *, bits_c, half):
    relations, slots = tiles_ref.shape[0], tiles_ref.shape[1]
    tile = tiles_ref.shape[2]
    panels = panel_ref.shape[0] // tile
    pieces = out_ref.shape[0] // relations
    height = out_ref.shape[2]
    my_row = lax.axis_index("rows")
    my_col = lax.axis_index("cols")
    for i in range(panels):
        turned_ref[i] = panel_ref[i * tile:(i + 1) * tile, :].T
    for k in range(relations):
        for s in range(slots):
            live = s < counts_ref[k, 0, 0]
            values = tiles_ref[k, s]
            values = jnp.where(live, values, jnp.zeros_like(values))
            col = cols_ref[k, 0, s] ^ my_row
            col = (col & 1) * half + (col >> 1)
            row = rows_ref[k, 0, s] ^ my_col
            upper_ref[:, s * tile:(s + 1) * tile] = dot(turned_ref[row], values).astype(jnp.bfloat16)
            picked_ref[s * tile:(s + 1) * tile, :] = factors_ref[col]
        core = dot(upper_ref[...], picked_ref[...])
        for p in range(pieces):
            place = reversed_slot((k * pieces + p) ^ my_col, bits_c)
            for h in range(2):
                begin = (2 * p + h) * height
                out_ref[place, h ^ (my_row & 1)] = core[begin:begin + height, :]


def second_pass(rows, cols, counts, tiles, factors, panel):
    relations, slots, tile, _ = tiles.shape
    rank = panel.shape[-1]
    n_rows, n_cols = lax.axis_size("rows"), lax.axis_size("cols")
    smem = pl.BlockSpec(memory_space=pltpu.SMEM)
    vmem = pl.BlockSpec(memory_space=pltpu.VMEM)
    return pl.pallas_call(
        functools.partial(second_kernel, bits_c=bits_of("cols"), half=n_rows // 2),
        out_shape=jax.ShapeDtypeStruct(
            (n_cols, 2, relations * rank // n_cols // 2, rank), jnp.float32
        ),
        in_specs=[smem, smem, smem, vmem, vmem, vmem],
        out_specs=vmem,
        scratch_shapes=[
            pltpu.VMEM((n_cols, rank, tile), jnp.bfloat16),
            pltpu.VMEM((rank, slots * tile), jnp.bfloat16),
            pltpu.VMEM((slots * tile, rank), jnp.bfloat16),
        ],
        compiler_params=params(),
        name="second_pass",
    )(rows, cols, counts, tiles, factors.reshape(n_rows, tile, rank), panel)


def order_kernel(in_ref, out_ref, *, bits_c):
    my_col = lax.axis_index("cols")
    my_row = lax.axis_index("rows")
    for j in range(out_ref.shape[0]):
        place = reversed_slot(j ^ my_col, bits_c)
        for h in range(2):
            out_ref[j, h] = in_ref[place, h ^ (my_row & 1)]


def in_order(x):
    return pl.pallas_call(
        functools.partial(order_kernel, bits_c=bits_of("cols")),
        out_shape=jax.ShapeDtypeStruct(x.shape, x.dtype),
        in_specs=[pl.BlockSpec(memory_space=pltpu.VMEM)],
        out_specs=pl.BlockSpec(memory_space=pltpu.VMEM),
        compiler_params=params(),
        name="in_order",
    )(x)


def sum_cols(x):
    for b in range(bits_of("cols")):
        x = x + swap(x, "cols", 1 << b)
    return x


def normal_system(summed_gram_matrix, cores_float32):
    direct_part = jnp.einsum(
        "krs,st,kqt->rq", cores_float32, summed_gram_matrix, cores_float32,
        precision=lax.Precision.HIGHEST,
    )
    reflected_part = jnp.einsum(
        "euh,uc,eca->ha", cores_float32, summed_gram_matrix, cores_float32,
        precision=lax.Precision.HIGHEST,
    )
    return (
        direct_part
        + reflected_part
        + ridge_weight * jnp.eye(summed_gram_matrix.shape[0], dtype=jnp.float32)
    )


def solve_rows(cholesky_lhs, numerator):
    halfway = lax.linalg.triangular_solve(cholesky_lhs, numerator.T, left_side=True, lower=True)
    return lax.linalg.triangular_solve(
        cholesky_lhs, halfway, left_side=True, lower=True, transpose_a=True
    ).T


def whiten(cholesky_new, core_num):
    relations, rank_size, _ = core_num.shape
    stacked = core_num.transpose(1, 0, 2).reshape(rank_size, relations * rank_size)
    halfway = lax.linalg.triangular_solve(cholesky_new, stacked, left_side=True, lower=True)
    flipped = (
        halfway.reshape(rank_size, relations, rank_size)
        .transpose(2, 1, 0)
        .reshape(rank_size, relations * rank_size)
    )
    second = lax.linalg.triangular_solve(cholesky_new, flipped, left_side=True, lower=True)
    return second.reshape(rank_size, relations, rank_size).transpose(1, 2, 0)


def local(factor, cores, tile_values, tile_rows, tile_cols, tile_counts):
    relations, slots, tile, _ = tile_values.shape
    rank = factor.shape[1]
    n_rows, n_cols = lax.axis_size("rows"), lax.axis_size("cols")
    half = n_rows // 2
    cores_float32 = cores.astype(jnp.float32)
    magnitude = jnp.abs(cores_float32)
    reach = jnp.maximum(jnp.max(jnp.sum(magnitude, 1)), jnp.max(jnp.sum(magnitude, 2)))
    scale = f16_top / (2.0 * n_cols * relations * slots * product_bound * reach + 1e-20)

    panel = gather_cols(factor)
    factors = gather_rows(factor)
    gram_old = sum_cols(dot(factors, factors, ((0,), (0,))))
    cholesky_lhs = jnp.linalg.cholesky(normal_system(gram_old, cores_float32))
    direct, back = first_pass(tile_rows, tile_cols, tile_counts, tile_values, factors, panel, cores)
    keep, give = back[:half], back[half:]
    back = keep + swap(half_of(give, scale), "rows", 1).astype(jnp.float32) / scale
    packed = half_of(back, scale)
    received = [swap(packed[i], "rows", 2 * i).astype(jnp.float32) for i in range(1, half)]
    numerator = (
        scatter_cols(direct, scale)[0] + back[0] + functools.reduce(jnp.add, received) / scale
    )
    factor_new = solve_rows(cholesky_lhs, numerator).astype(jnp.bfloat16)

    panel_new = gather_cols(factor_new)
    factors_new = gather_rows(factor_new)
    gram_new = sum_cols(dot(factors_new, factors_new, ((0,), (0,))))
    lower_new = jnp.linalg.cholesky(gram_new)
    longest = jnp.max(jnp.diagonal(gram_new))
    tiles_in_all = n_rows * n_cols
    scale_core = f16_top / (2.0 * slots * tile * value_bound * tiles_in_all * longest + 1e-30)
    core = second_pass(tile_rows, tile_cols, tile_counts, tile_values, factors_new, panel_new)
    core = scatter_cols(core, scale_core)[0]
    core = core[0] + swap(half_of(core[1], scale_core), "rows", 1).astype(jnp.float32) / scale_core
    packed = half_of(core, scale_core)
    core = tree_sum(
        [packed.astype(jnp.float32)]
        + [swap(packed, "rows", 2 * i).astype(jnp.float32) for i in range(1, half)]
    )
    core = core.astype(jnp.float16)[None]
    core = jnp.concatenate([core, swap(core, "rows", 1)], axis=0)[None]
    for b in reversed(range(bits_of("cols"))):
        core = jnp.concatenate([core, swap(core, "cols", 1 << b)], axis=0)
    core = in_order(core.astype(jnp.float32)) / scale_core
    core_num = core.reshape(relations, rank, rank)
    cores_new = whiten(lower_new, core_num)
    return (factor_new, cores_new)


def solution(mesh):
    in_specs = (
        P(("rows", "cols"), None),
        P(),
        P(None, "rows", "cols", None),
        P(None, "rows", "cols"),
        P(None, "rows", "cols"),
        P(None, "rows", "cols"),
    )
    out_specs = (P(("rows", "cols"), None), P())
    return jax.shard_map(local, mesh=mesh, in_specs=in_specs, out_specs=out_specs, check_vma=False)
```

```python
import functools

import jax
import jax.numpy as jnp
from jax import lax
from jax.experimental import pallas as pl
from jax.experimental.pallas import tpu as pltpu
from jax.sharding import PartitionSpec as P

ridge_weight = 0.1
value_bound = 160.0
product_bound = 672.0
f16_top = 30000.0


def params():
    return pltpu.CompilerParams(vmem_limit_bytes=48 * 1024 * 1024)


def swap(x, axis, mask):
    size = lax.axis_size(axis)
    return lax.ppermute(x, axis, [(i, i ^ mask) for i in range(size)])


def bits_of(axis):
    return lax.axis_size(axis).bit_length() - 1


def reversed_slot(slot, bits):
    out = 0
    for b in range(bits):
        out = out + (((slot >> b) & 1) << (bits - 1 - b))
    return out


def gather_cols(x):
    pieces = [x]
    for b in range(bits_of("cols")):
        pieces = pieces + [swap(p, "cols", 1 << b) for p in pieces]
    return pieces


def gather_rows(x):
    half = lax.axis_size("rows") // 2
    even = [x] + [swap(x, "rows", 2 * i) for i in range(1, half)]
    return even + [swap(p, "rows", 1) for p in even]


def tree_sum(parts):
    while len(parts) > 1:
        parts = [parts[i] + parts[i + 1] for i in range(0, len(parts), 2)]
    return parts[0]


def half_of(x, scale):
    return (x * scale).astype(jnp.float16)


def scatter_cols(x, scale):
    for b in range(bits_of("cols")):
        keep, give = jnp.split(x, 2, axis=0)
        if b == 0:
            x = keep + swap(give, "cols", 1)
        else:
            x = keep + swap(half_of(give, scale), "cols", 1 << b).astype(jnp.float32) / scale
    return x


def dot(a, b, dims=((1,), (0,)), precision=None):
    return lax.dot_general(
        a, b, (dims, ((), ())), preferred_element_type=jnp.float32, precision=precision
    )


def gram_kernel(*refs):
    pieces, factors_ref, gram_ref = refs[:-2], refs[-2], refs[-1]
    tile = pieces[0].shape[0]
    for i, piece in enumerate(pieces):
        factors_ref[i * tile:(i + 1) * tile, :] = piece[...]
    whole = factors_ref[...]
    gram = dot(whole, whole, ((0,), (0,)))
    side = gram_ref.shape[1]
    gram_ref[0] = gram[:side, :side]
    gram_ref[1] = gram[:side, side:]
    gram_ref[2] = gram[side:, side:]


def gram_of(pieces):
    tile, rank = pieces[0].shape
    vmem = pl.BlockSpec(memory_space=pltpu.VMEM)
    factors, gram = pl.pallas_call(
        gram_kernel,
        out_shape=(
            jax.ShapeDtypeStruct((len(pieces) * tile, rank), jnp.bfloat16),
            jax.ShapeDtypeStruct((3, rank // 2, rank // 2), jnp.float32),
        ),
        in_specs=[vmem] * len(pieces),
        out_specs=(vmem, vmem),
        compiler_params=params(),
        name="gram",
    )(*pieces)
    return factors, gram


def first_kernel(rows_ref, cols_ref, counts_ref, tiles_ref, factors_ref, cores_ref, *refs,
                 bits_c, half):
    panel_refs = refs[:-5]
    direct_ref, back_ref, acc_ref, turned_ref, sums_ref = refs[-5:]
    relations, slots = tiles_ref.shape[0], tiles_ref.shape[1]
    tile = tiles_ref.shape[2]
    panels = len(panel_refs)
    my_row = lax.axis_index("rows")
    my_col = lax.axis_index("cols")
    sums_ref[...] = jnp.zeros_like(sums_ref)
    for k in range(relations):
        core = cores_ref[k]
        for i in range(panels):
            rotated = dot(panel_refs[i][...], core).astype(jnp.bfloat16)
            turned_ref[i] = rotated.T
        acc_ref[...] = jnp.zeros_like(acc_ref)
        for s in range(slots):
            live = s < counts_ref[k, 0, 0]
            values = tiles_ref[k, s]
            values = jnp.where(live, values, jnp.zeros_like(values))
            col = cols_ref[k, 0, s] ^ my_row
            col = (col & 1) * half + (col >> 1)
            row = rows_ref[k, 0, s] ^ my_col
            acc_ref[row] += dot(values, factors_ref[col])
            sums_ref[col] += dot(turned_ref[row], values)
        for i in range(panels):
            whole = acc_ref[i]
            high = whole.astype(jnp.bfloat16)
            low = (whole - high.astype(jnp.float32)).astype(jnp.bfloat16)
            part = dot(high, core, ((1,), (1,))) + dot(low, core, ((1,), (1,)))
            place = reversed_slot(i, bits_c)
            if k == 0:
                direct_ref[place] = part
            else:
                direct_ref[place] += part
    for g in range(sums_ref.shape[0]):
        back_ref[g] = sums_ref[g].T


def first_pass(rows, cols, counts, tiles, factors, panel, cores):
    relations, slots, tile, _ = tiles.shape
    rank = cores.shape[-1]
    n_rows, n_cols = lax.axis_size("rows"), lax.axis_size("cols")
    smem = pl.BlockSpec(memory_space=pltpu.SMEM)
    vmem = pl.BlockSpec(memory_space=pltpu.VMEM)
    return pl.pallas_call(
        functools.partial(first_kernel, bits_c=bits_of("cols"), half=n_rows // 2),
        out_shape=(
            jax.ShapeDtypeStruct((n_cols, tile, rank), jnp.float32),
            jax.ShapeDtypeStruct((n_rows, tile, rank), jnp.float32),
        ),
        in_specs=[smem, smem, smem, vmem, vmem, vmem] + [vmem] * len(panel),
        out_specs=(vmem, vmem),
        scratch_shapes=[
            pltpu.VMEM((n_cols, tile, rank), jnp.float32),
            pltpu.VMEM((n_cols, rank, tile), jnp.bfloat16),
            pltpu.VMEM((n_rows, rank, tile), jnp.float32),
        ],
        compiler_params=params(),
        name="first_pass",
    )(rows, cols, counts, tiles, factors.reshape(n_rows, tile, rank), cores, *panel)


def second_kernel(rows_ref, cols_ref, counts_ref, tiles_ref, factors_ref, *refs, bits_c, half):
    panel_refs = refs[:-4]
    out_ref, turned_ref, upper_ref, picked_ref = refs[-4:]
    relations, slots = tiles_ref.shape[0], tiles_ref.shape[1]
    tile = tiles_ref.shape[2]
    panels = len(panel_refs)
    pieces = out_ref.shape[0] // relations
    height = out_ref.shape[2]
    my_row = lax.axis_index("rows")
    my_col = lax.axis_index("cols")
    for i in range(panels):
        turned_ref[i] = panel_refs[i][...].T
    for k in range(relations):
        for s in range(slots):
            live = s < counts_ref[k, 0, 0]
            values = tiles_ref[k, s]
            values = jnp.where(live, values, jnp.zeros_like(values))
            col = cols_ref[k, 0, s] ^ my_row
            col = (col & 1) * half + (col >> 1)
            row = rows_ref[k, 0, s] ^ my_col
            upper_ref[:, s * tile:(s + 1) * tile] = dot(turned_ref[row], values).astype(jnp.bfloat16)
            picked_ref[s * tile:(s + 1) * tile, :] = factors_ref[col]
        core = dot(upper_ref[...], picked_ref[...])
        for p in range(pieces):
            place = reversed_slot((k * pieces + p) ^ my_col, bits_c)
            for h in range(2):
                begin = (2 * p + h) * height
                out_ref[place, h ^ (my_row & 1)] = core[begin:begin + height, :]


def second_pass(rows, cols, counts, tiles, factors, panel):
    relations, slots, tile, _ = tiles.shape
    rank = panel[0].shape[-1]
    n_rows, n_cols = lax.axis_size("rows"), lax.axis_size("cols")
    smem = pl.BlockSpec(memory_space=pltpu.SMEM)
    vmem = pl.BlockSpec(memory_space=pltpu.VMEM)
    return pl.pallas_call(
        functools.partial(second_kernel, bits_c=bits_of("cols"), half=n_rows // 2),
        out_shape=jax.ShapeDtypeStruct(
            (n_cols, 2, relations * rank // n_cols // 2, rank), jnp.float32
        ),
        in_specs=[smem, smem, smem, vmem, vmem] + [vmem] * len(panel),
        out_specs=vmem,
        scratch_shapes=[
            pltpu.VMEM((n_cols, rank, tile), jnp.bfloat16),
            pltpu.VMEM((rank, slots * tile), jnp.bfloat16),
            pltpu.VMEM((slots * tile, rank), jnp.bfloat16),
        ],
        compiler_params=params(),
        name="second_pass",
    )(rows, cols, counts, tiles, factors.reshape(n_rows, tile, rank), *panel)


def split(x, terms):
    parts = []
    for _ in range(terms):
        part = x.astype(jnp.bfloat16)
        parts.append(part)
        x = x - part.astype(jnp.float32)
    return parts


def eliminate(z_ref, begin, end, block, sub):
    size = z_ref.shape[0]
    wide = size // 128
    for p in range(begin, end):
        o = p * block
        panel = z_ref[o:o + block, :]
        rows = lax.broadcasted_iota(jnp.int32, (block, 128), 0)
        rows_wide = lax.broadcasted_iota(jnp.int32, (block, size), 0)
        lanes = lax.broadcasted_iota(jnp.int32, (block, size), 1)
        for q in range(block // sub):
            first = o + q * sub
            cols = [
                jnp.broadcast_to(panel[:, first + m:first + m + 1], (block, 128))
                for m in range(sub)
            ]
            for m in range(sub):
                j = q * sub + m
                root = lax.rsqrt(cols[m][j:j + 1, :])
                factors = jnp.where(rows > j, cols[m] * root, 0.0)
                for t in range(m + 1, sub):
                    cols[t] = cols[t] - factors * (cols[t][j:j + 1, :] * root)
                unit = jnp.where(rows_wide == j, 1.0, 0.0)
                panel = jnp.where(lanes == o + j, unit, panel)
                line = panel[j:j + 1, :] * jnp.concatenate([root] * wide, axis=1)
                factors = jnp.concatenate([factors] * wide, axis=1)
                panel = jnp.where(rows_wide == j, line, panel - factors * line)
        z_ref[o:o + block, :] = panel
        rest = size - o - block
        if rest:
            high, mid, low = split(panel, 3)
            left = jnp.concatenate([high, high, mid, mid, high, low], axis=0)[:, o + block:]
            right = jnp.concatenate([high, mid, high, mid, low, high], axis=0)
            change = dot(left, right, ((0,), (0,)))
            lanes = lax.broadcasted_iota(jnp.int32, (rest, size), 1)
            done = (lanes >= o) & (lanes < o + block)
            z_ref[o + block:, :] = jnp.where(done, 0.0, z_ref[o + block:, :]) - change


def lower_of(z):
    rows = lax.broadcasted_iota(jnp.int32, z.shape, 0)
    lanes = lax.broadcasted_iota(jnp.int32, z.shape, 1)
    return jnp.where(rows >= lanes, z, 0.0)


def system_kernel(mine_ref, other_ref, cores_ref, out_ref, z_ref):
    size = z_ref.shape[0]
    side = size // 2
    upper = mine_ref[1] + other_ref[1]
    z_ref[:side, :side] = mine_ref[0] + other_ref[0]
    z_ref[:side, side:] = upper
    z_ref[side:, :side] = upper.T
    z_ref[side:, side:] = mine_ref[2] + other_ref[2]
    grams = jnp.concatenate(split(z_ref[...], 3), axis=0)
    rows = lax.broadcasted_iota(jnp.int32, (size, size), 0)
    lanes = lax.broadcasted_iota(jnp.int32, (size, size), 1)
    total = jnp.where(rows == lanes, ridge_weight, 0.0)
    for k in range(cores_ref.shape[0]):
        core = cores_ref[k]
        turned = core.T
        for left, right in ((core, turned), (turned, core)):
            middle = dot(jnp.concatenate([left] * 3, axis=1), grams)
            middle = jnp.concatenate(split(middle, 3), axis=1)
            total = total + dot(middle, jnp.concatenate([right] * 3, axis=0))
    z_ref[...] = total
    eliminate(z_ref, 0, size // 32, 32, 16)
    lower = lower_of(z_ref[...])
    high, mid, low = split(lower, 3)
    left = jnp.concatenate([high, high, mid, mid, high, low], axis=0)
    right = jnp.concatenate([high, mid, high, mid, low, high], axis=0)
    out_ref[...] = dot(left, right, ((0,), (0,)))


def system_inverse(mine, other, cores):
    rank = cores.shape[-1]
    vmem = pl.BlockSpec(memory_space=pltpu.VMEM)
    return pl.pallas_call(
        system_kernel,
        out_shape=jax.ShapeDtypeStruct((rank, rank), jnp.float32),
        in_specs=[vmem] * 3,
        out_specs=vmem,
        scratch_shapes=[pltpu.VMEM((rank, rank), jnp.float32)],
        compiler_params=params(),
        cost_estimate=pl.CostEstimate(flops=9_000_000_000, bytes_accessed=1_500_000, transcendentals=0),
        name="system_inverse",
    )(mine, other, cores)


def begin_kernel(mine_ref, other_ref, out_ref):
    size = out_ref.shape[0]
    side = size // 2
    out_ref[:side, :side] = mine_ref[0] + other_ref[0]
    out_ref[:side, side:] = mine_ref[1] + other_ref[1]
    out_ref[side:, :side] = jnp.zeros((side, side), jnp.float32)
    out_ref[side:, side:] = mine_ref[2] + other_ref[2]
    eliminate(out_ref, 0, size // 64, 32, 16)


def end_kernel(in_ref, out_ref):
    size = out_ref.shape[0]
    out_ref[...] = in_ref[...]
    eliminate(out_ref, size // 64, size // 32, 32, 16)


def half_eliminate(kernel, name, rank, *args):
    vmem = pl.BlockSpec(memory_space=pltpu.VMEM)
    return pl.pallas_call(
        kernel,
        out_shape=jax.ShapeDtypeStruct((rank, rank), jnp.float32),
        in_specs=[vmem] * len(args),
        out_specs=vmem,
        compiler_params=params(),
        cost_estimate=pl.CostEstimate(flops=3_500_000_000, bytes_accessed=500_000, transcendentals=0),
        name=name,
    )(*args)


def whiten_kernel(z_ref, factor_ref, near_ref, far_ref, out_ref, core_ref, *, bits_c):
    relations, rank = out_ref.shape[0], out_ref.shape[1]
    halves = near_ref.shape[0]
    pieces = 2 * halves // relations
    height = near_ref.shape[2]
    my_col = lax.axis_index("cols")
    my_row = lax.axis_index("rows")
    core_ref[:halves] = near_ref[...]
    core_ref[halves:] = far_ref[...]
    high, low = split(lower_of(z_ref[...]), 2)
    left = jnp.concatenate([high, high, low], axis=1)
    right = jnp.concatenate([high, low, high], axis=1)
    for k in range(relations):
        parts = []
        for p in range(pieces):
            place = reversed_slot((k * pieces + p) ^ my_col, bits_c)
            parts += [core_ref[place, h ^ (my_row & 1)] for h in range(2)]
        core = jnp.concatenate(parts, axis=0) * factor_ref[0]
        first, rest = split(core, 2)
        middle = dot(left, jnp.concatenate([first, rest, first], axis=0))
        first, rest = split(middle, 2)
        out_ref[k] = dot(jnp.concatenate([first, first, rest], axis=1), right, ((1,), (1,)))


def whiten(z, factor, near, far, relations):
    rank = z.shape[0]
    vmem = pl.BlockSpec(memory_space=pltpu.VMEM)
    return pl.pallas_call(
        functools.partial(whiten_kernel, bits_c=bits_of("cols")),
        out_shape=jax.ShapeDtypeStruct((relations, rank, rank), jnp.float32),
        in_specs=[vmem, pl.BlockSpec(memory_space=pltpu.SMEM), vmem, vmem],
        out_specs=vmem,
        scratch_shapes=[pltpu.VMEM((2 * near.shape[0],) + near.shape[1:], jnp.float32)],
        compiler_params=params(),
        name="whiten",
    )(z, factor.reshape(1), near, far)


def pair_of_sums(x):
    for b in range(bits_of("cols") - 1):
        x = x + swap(x, "cols", 1 << b)
    return x, swap(x, "cols", 1 << (bits_of("cols") - 1))


def local(factor, cores, tile_values, tile_rows, tile_cols, tile_counts):
    relations, slots, tile, _ = tile_values.shape
    rank = factor.shape[1]
    n_rows, n_cols = lax.axis_size("rows"), lax.axis_size("cols")
    half = n_rows // 2
    magnitude = jnp.abs(cores.astype(jnp.float32))
    reach = jnp.maximum(jnp.max(jnp.sum(magnitude, 1)), jnp.max(jnp.sum(magnitude, 2)))
    scale = f16_top / (2.0 * n_cols * relations * slots * product_bound * reach + 1e-20)

    factors, gram = gram_of(gather_rows(factor))
    panel = gather_cols(factor)
    gram_pair = pair_of_sums(gram)
    direct, back = first_pass(tile_rows, tile_cols, tile_counts, tile_values, factors, panel, cores)
    inverse = system_inverse(*gram_pair, cores)
    parts = []
    for begin in range(half, 0, -half // 2):
        begin = begin - half // 2
        end = begin + half // 2
        give = half_of(back[half + begin:half + end], scale)
        parts = [back[begin:end] + swap(give, "rows", 1).astype(jnp.float32) / scale] + parts
    packed = [half_of(part, scale) for part in parts]
    received = [
        swap(packed[i // (half // 2)][i % (half // 2)], "rows", 2 * i).astype(jnp.float32)
        for i in range(1, half)
    ]
    numerator = (
        scatter_cols(direct, scale)[0] + parts[0][0] + functools.reduce(jnp.add, received) / scale
    )
    factor_new = dot(numerator, inverse, precision=lax.Precision.HIGHEST).astype(jnp.bfloat16)

    factors_new, gram_new = gram_of(gather_rows(factor_new))
    panel_new = gather_cols(factor_new)
    gram_pair = pair_of_sums(gram_new)
    longest = jnp.max(gram_pair[0] + gram_pair[1])
    tiles_in_all = n_rows * n_cols
    scale_core = f16_top / (2.0 * slots * tile * value_bound * tiles_in_all * longest + 1e-30)
    core = second_pass(tile_rows, tile_cols, tile_counts, tile_values, factors_new, panel_new)
    core = scatter_cols(core, scale_core)[0]
    z = half_eliminate(begin_kernel, "begin", rank, *gram_pair)
    core = core[0] + swap(half_of(core[1], scale_core), "rows", 1).astype(jnp.float32) / scale_core
    packed = half_of(core, scale_core)
    core = tree_sum(
        [packed.astype(jnp.float32)]
        + [swap(packed, "rows", 2 * i).astype(jnp.float32) for i in range(1, half)]
    )
    z = half_eliminate(end_kernel, "end", rank, z)
    core = core.astype(jnp.float16)[None]
    core = jnp.concatenate([core, swap(core, "rows", 1)], axis=0)[None]
    for b in reversed(range(1, bits_of("cols"))):
        core = jnp.concatenate([core, swap(core, "cols", 1 << b)], axis=0)
    far = swap(core, "cols", 1)
    cores_new = whiten(
        z, 1.0 / scale_core, core.astype(jnp.float32), far.astype(jnp.float32), relations
    )
    return (factor_new, cores_new)


def solution(mesh):
    in_specs = (
        P(("rows", "cols"), None),
        P(),
        P(None, "rows", "cols", None),
        P(None, "rows", "cols"),
        P(None, "rows", "cols"),
        P(None, "rows", "cols"),
    )
    out_specs = (P(("rows", "cols"), None), P())
    return jax.shard_map(local, mesh=mesh, in_specs=in_specs, out_specs=out_specs, check_vma=False)
```

```python
import functools

import jax
import jax.numpy as jnp
from jax import lax
from jax.experimental import pallas as pl
from jax.experimental.pallas import tpu as pltpu
from jax.sharding import PartitionSpec as P

ridge_weight = 0.1
value_bound = 160.0
product_bound = 672.0
f16_top = 30000.0


def params():
    return pltpu.CompilerParams(vmem_limit_bytes=48 * 1024 * 1024)


def swap(x, axis, mask):
    size = lax.axis_size(axis)
    return lax.ppermute(x, axis, [(i, i ^ mask) for i in range(size)])


def swap_both(x, row_mask, col_mask):
    if col_mask == 0:
        return swap(x, "rows", row_mask)
    if row_mask == 0:
        return swap(x, "cols", col_mask)
    n_cols = lax.axis_size("cols")
    mask = row_mask * n_cols + col_mask
    size = lax.axis_size("rows") * n_cols
    return lax.ppermute(x, ("rows", "cols"), [(i, i ^ mask) for i in range(size)])


def cost(microseconds):
    return pl.CostEstimate(
        flops=int(microseconds * 1.1e9), bytes_accessed=100_000, transcendentals=0
    )


def after(x, other):
    return lax.optimization_barrier((x, other))[0]


def bits_of(axis):
    return lax.axis_size(axis).bit_length() - 1


def reversed_slot(slot, bits):
    out = 0
    for b in range(bits):
        out = out + (((slot >> b) & 1) << (bits - 1 - b))
    return out


def gather_cols(x):
    for b in range(bits_of("cols")):
        x = jnp.concatenate([x, swap(x, "cols", 1 << b)], axis=0)
    return x


def gather_rows(x):
    half = lax.axis_size("rows") // 2
    across = swap(x, "rows", 1)
    even = [swap(x, "rows", 2 * i) for i in range(1, half)]
    middle = half // 2
    odd = [
        swap(jnp.concatenate(part, axis=0), "rows", 1) for part in (even[:middle], even[middle:])
    ]
    return [x] + even + [across] + odd


def tree_sum(parts):
    while len(parts) > 1:
        parts = [parts[i] + parts[i + 1] for i in range(0, len(parts), 2)]
    return parts[0]


def half_of(x, scale):
    return (x * scale).astype(jnp.float16)


def scatter_cols(x, scale):
    for b in range(bits_of("cols")):
        keep, give = jnp.split(x, 2, axis=0)
        if b == 0:
            x = keep + swap(give, "cols", 1)
        else:
            x = keep + swap(half_of(give, scale), "cols", 1 << b).astype(jnp.float32) / scale
    return x


def dot(a, b, dims=((1,), (0,)), precision=None):
    return lax.dot_general(
        a, b, (dims, ((), ())), preferred_element_type=jnp.float32, precision=precision
    )


def gram_kernel(*refs):
    pieces, factors_ref, gram_ref = refs[:-2], refs[-2], refs[-1]
    begin = 0
    for piece in pieces:
        factors_ref[begin:begin + piece.shape[0], :] = piece[...]
        begin += piece.shape[0]
    whole = factors_ref[...]
    gram = dot(whole, whole, ((0,), (0,)))
    side = gram_ref.shape[1]
    gram_ref[0] = gram[:side, :side]
    gram_ref[1] = gram[:side, side:]
    gram_ref[2] = gram[side:, side:]


def gram_of(pieces):
    rank = pieces[0].shape[1]
    height = sum(piece.shape[0] for piece in pieces)
    vmem = pl.BlockSpec(memory_space=pltpu.VMEM)
    factors, gram = pl.pallas_call(
        gram_kernel,
        out_shape=(
            jax.ShapeDtypeStruct((height, rank), jnp.bfloat16),
            jax.ShapeDtypeStruct((3, rank // 2, rank // 2), jnp.float32),
        ),
        in_specs=[vmem] * len(pieces),
        out_specs=(vmem, vmem),
        compiler_params=params(),
        cost_estimate=cost(0.4),
        name="gram",
    )(*pieces)
    return factors, gram


def prepare_kernel(rows_ref, cols_ref, counts_ref, tiles_ref, cores_ref, factor_ref,
                   places_ref, scale_ref, live_ref, copied_ref, own_ref, *, half, terms):
    relations, slots = tiles_ref.shape[0], tiles_ref.shape[1]
    my_row = lax.axis_index("rows")
    my_col = lax.axis_index("cols")
    own_ref[...] = factor_ref[...]
    reach = jnp.zeros((1, 1), jnp.float32)
    for k in range(relations):
        core = cores_ref[k]
        copied_ref[k] = core
        size = jnp.abs(core.astype(jnp.float32))
        for axis in (0, 1):
            sums = jnp.sum(size, axis=axis, keepdims=True)
            reach = jnp.maximum(reach, jnp.max(sums, axis=1 - axis, keepdims=True))
        for s in range(slots):
            live = s < counts_ref[k, 0, 0]
            values = tiles_ref[k, s]
            live_ref[k, s] = jnp.where(live, values, jnp.zeros_like(values))
            col = cols_ref[k, 0, s] ^ my_row
            places_ref[k, s] = (col & 1) * half + (col >> 1)
            places_ref[k, slots + s] = rows_ref[k, 0, s] ^ my_col
    scale_ref[...] = jnp.broadcast_to(
        f16_top / (terms * relations * slots * product_bound * reach + 1e-20), scale_ref.shape
    )


def prepare(rows, cols, counts, tiles, cores, factor):
    n_rows, n_cols = lax.axis_size("rows"), lax.axis_size("cols")
    smem = pl.BlockSpec(memory_space=pltpu.SMEM)
    vmem = pl.BlockSpec(memory_space=pltpu.VMEM)
    return pl.pallas_call(
        functools.partial(prepare_kernel, half=n_rows // 2, terms=2.0 * n_cols),
        out_shape=(
            jax.ShapeDtypeStruct((tiles.shape[0], 2 * tiles.shape[1]), jnp.int32),
            jax.ShapeDtypeStruct((8, 128), jnp.float32),
            jax.ShapeDtypeStruct(tiles.shape, tiles.dtype),
            jax.ShapeDtypeStruct(cores.shape, cores.dtype),
            jax.ShapeDtypeStruct(factor.shape, factor.dtype),
        ),
        in_specs=[smem, smem, smem, vmem, vmem, vmem],
        out_specs=(smem, vmem, vmem, vmem, vmem),
        compiler_params=params(),
        cost_estimate=cost(2.0),
        name="prepare",
    )(rows, cols, counts, tiles, cores, factor)


def first_kernel(places_ref, tiles_ref, factors_ref, panel_ref, cores_ref,
                 direct_ref, back_ref, acc_ref, turned_ref, sums_ref, *, bits_c):
    relations, slots = tiles_ref.shape[0], tiles_ref.shape[1]
    tile = tiles_ref.shape[2]
    panels = panel_ref.shape[0] // tile
    sums_ref[...] = jnp.zeros_like(sums_ref)
    for k in range(relations):
        core = cores_ref[k]
        for i in range(panels):
            rotated = dot(panel_ref[i * tile:(i + 1) * tile, :], core).astype(jnp.bfloat16)
            turned_ref[i] = rotated.T
        acc_ref[...] = jnp.zeros_like(acc_ref)
        for s in range(slots):
            values = tiles_ref[k, s]
            col = places_ref[k, s]
            row = places_ref[k, slots + s]
            acc_ref[row] += dot(values, factors_ref[col])
            sums_ref[col] += dot(turned_ref[row], values)
        for i in range(panels):
            whole = acc_ref[i]
            high = whole.astype(jnp.bfloat16)
            low = (whole - high.astype(jnp.float32)).astype(jnp.bfloat16)
            part = dot(high, core, ((1,), (1,))) + dot(low, core, ((1,), (1,)))
            place = reversed_slot(i, bits_c)
            if k == 0:
                direct_ref[place] = part
            else:
                direct_ref[place] += part
    for g in range(sums_ref.shape[0]):
        back_ref[g] = sums_ref[g].T


def first_pass(places, tiles, factors, panel, cores):
    tile = tiles.shape[2]
    rank = cores.shape[-1]
    n_rows, n_cols = lax.axis_size("rows"), lax.axis_size("cols")
    smem = pl.BlockSpec(memory_space=pltpu.SMEM)
    vmem = pl.BlockSpec(memory_space=pltpu.VMEM)
    return pl.pallas_call(
        functools.partial(first_kernel, bits_c=bits_of("cols")),
        out_shape=(
            jax.ShapeDtypeStruct((n_cols, tile, rank), jnp.float32),
            jax.ShapeDtypeStruct((n_rows, tile, rank), jnp.float32),
        ),
        in_specs=[smem, vmem, vmem, vmem, vmem],
        out_specs=(vmem, vmem),
        scratch_shapes=[
            pltpu.VMEM((n_cols, tile, rank), jnp.float32),
            pltpu.VMEM((n_cols, rank, tile), jnp.bfloat16),
            pltpu.VMEM((n_rows, rank, tile), jnp.float32),
        ],
        compiler_params=params(),
        cost_estimate=cost(4.8),
        name="first_pass",
    )(places, tiles, factors.reshape(n_rows, tile, rank), panel, cores)


def second_kernel(places_ref, tiles_ref, factors_ref, panel_ref,
                  out_ref, turned_ref, upper_ref, picked_ref, *, bits_c):
    relations, slots = tiles_ref.shape[0], tiles_ref.shape[1]
    tile = tiles_ref.shape[2]
    panels = panel_ref.shape[0] // tile
    pieces = out_ref.shape[0] // relations
    height = out_ref.shape[2]
    my_row = lax.axis_index("rows")
    my_col = lax.axis_index("cols")
    for i in range(panels):
        turned_ref[i] = panel_ref[i * tile:(i + 1) * tile, :].T
    for k in range(relations):
        for s in range(slots):
            values = tiles_ref[k, s]
            col = places_ref[k, s]
            row = places_ref[k, slots + s]
            upper_ref[:, s * tile:(s + 1) * tile] = dot(turned_ref[row], values).astype(jnp.bfloat16)
            picked_ref[s * tile:(s + 1) * tile, :] = factors_ref[col]
        core = dot(upper_ref[...], picked_ref[...])
        for p in range(pieces):
            place = reversed_slot((k * pieces + p) ^ my_col, bits_c)
            for h in range(2):
                begin = (2 * p + h) * height
                out_ref[place, h ^ (my_row & 1)] = core[begin:begin + height, :]


def second_pass(places, tiles, factors, panel):
    relations, slots, tile, _ = tiles.shape
    rank = panel.shape[-1]
    n_rows, n_cols = lax.axis_size("rows"), lax.axis_size("cols")
    smem = pl.BlockSpec(memory_space=pltpu.SMEM)
    vmem = pl.BlockSpec(memory_space=pltpu.VMEM)
    return pl.pallas_call(
        functools.partial(second_kernel, bits_c=bits_of("cols")),
        out_shape=jax.ShapeDtypeStruct(
            (n_cols, 2, relations * rank // n_cols // 2, rank), jnp.float32
        ),
        in_specs=[smem, vmem, vmem, vmem],
        out_specs=vmem,
        scratch_shapes=[
            pltpu.VMEM((n_cols, rank, tile), jnp.bfloat16),
            pltpu.VMEM((rank, slots * tile), jnp.bfloat16),
            pltpu.VMEM((slots * tile, rank), jnp.bfloat16),
        ],
        compiler_params=params(),
        cost_estimate=cost(2.8),
        name="second_pass",
    )(places, tiles, factors.reshape(n_rows, tile, rank), panel)


def split(x, terms):
    parts = []
    for _ in range(terms):
        part = x.astype(jnp.bfloat16)
        parts.append(part)
        x = x - part.astype(jnp.float32)
    return parts


def eliminate(z_ref, begin, end, block, sub):
    size = z_ref.shape[0]
    wide = size // 128
    for p in range(begin, end):
        o = p * block
        panel = z_ref[o:o + block, :]
        rows = lax.broadcasted_iota(jnp.int32, (block, 128), 0)
        rows_wide = lax.broadcasted_iota(jnp.int32, (block, size), 0)
        lanes = lax.broadcasted_iota(jnp.int32, (block, size), 1)
        for q in range(block // sub):
            first = o + q * sub
            cols = [
                jnp.broadcast_to(panel[:, first + m:first + m + 1], (block, 128))
                for m in range(sub)
            ]
            for m in range(sub):
                j = q * sub + m
                root = lax.rsqrt(cols[m][j:j + 1, :])
                factors = jnp.where(rows > j, cols[m] * root, 0.0)
                for t in range(m + 1, sub):
                    cols[t] = cols[t] - factors * (cols[t][j:j + 1, :] * root)
                unit = jnp.where(rows_wide == j, 1.0, 0.0)
                panel = jnp.where(lanes == o + j, unit, panel)
                line = panel[j:j + 1, :] * jnp.concatenate([root] * wide, axis=1)
                factors = jnp.concatenate([factors] * wide, axis=1)
                panel = jnp.where(rows_wide == j, line, panel - factors * line)
        z_ref[o:o + block, :] = panel
        rest = size - o - block
        if rest:
            high, mid, low = split(panel, 3)
            left = jnp.concatenate([high, high, mid, mid, high, low], axis=0)[:, o + block:]
            right = jnp.concatenate([high, mid, high, mid, low, high], axis=0)
            change = dot(left, right, ((0,), (0,)))
            lanes = lax.broadcasted_iota(jnp.int32, (rest, size), 1)
            done = (lanes >= o) & (lanes < o + block)
            z_ref[o + block:, :] = jnp.where(done, 0.0, z_ref[o + block:, :]) - change


def lower_of(z):
    rows = lax.broadcasted_iota(jnp.int32, z.shape, 0)
    lanes = lax.broadcasted_iota(jnp.int32, z.shape, 1)
    return jnp.where(rows >= lanes, z, 0.0)


def system_kernel(mine_ref, other_ref, cores_ref, z_ref):
    size = z_ref.shape[0]
    side = size // 2
    upper = mine_ref[1] + other_ref[1]
    z_ref[:side, :side] = mine_ref[0] + other_ref[0]
    z_ref[:side, side:] = upper
    z_ref[side:, :side] = upper.T
    z_ref[side:, side:] = mine_ref[2] + other_ref[2]
    grams = jnp.concatenate(split(z_ref[...], 3), axis=0)
    rows = lax.broadcasted_iota(jnp.int32, (size, size), 0)
    lanes = lax.broadcasted_iota(jnp.int32, (size, size), 1)
    total = jnp.where(rows == lanes, ridge_weight, 0.0)
    for k in range(cores_ref.shape[0]):
        core = cores_ref[k]
        turned = core.T
        for left, right in ((core, turned), (turned, core)):
            middle = dot(jnp.concatenate([left] * 3, axis=1), grams)
            middle = jnp.concatenate(split(middle, 3), axis=1)
            total = total + dot(middle, jnp.concatenate([right] * 3, axis=0))
    z_ref[...] = total
    eliminate(z_ref, 0, size // 128, 32, 16)


def inverse_kernel(in_ref, out_ref, z_ref):
    size = z_ref.shape[0]
    z_ref[...] = in_ref[...]
    eliminate(z_ref, size // 128, size // 32, 32, 16)
    high, mid, low = split(lower_of(z_ref[...]), 3)
    left = jnp.concatenate([high, high, mid, mid, high, low], axis=0)
    right = jnp.concatenate([high, mid, high, mid, low, high], axis=0)
    out_ref[...] = dot(left, right, ((0,), (0,)))


def begin_kernel(mine_ref, other_ref, out_ref):
    size = out_ref.shape[0]
    side = size // 2
    out_ref[:side, :side] = mine_ref[0] + other_ref[0]
    out_ref[:side, side:] = mine_ref[1] + other_ref[1]
    out_ref[side:, :side] = jnp.zeros((side, side), jnp.float32)
    out_ref[side:, side:] = mine_ref[2] + other_ref[2]
    eliminate(out_ref, 0, size // 64, 32, 16)


def end_kernel(in_ref, out_ref):
    size = out_ref.shape[0]
    out_ref[...] = in_ref[...]
    eliminate(out_ref, size // 64, size // 32, 32, 16)


def square_call(kernel, name, microseconds, rank, *args, scratch=False):
    vmem = pl.BlockSpec(memory_space=pltpu.VMEM)
    return pl.pallas_call(
        kernel,
        out_shape=jax.ShapeDtypeStruct((rank, rank), jnp.float32),
        in_specs=[vmem] * len(args),
        out_specs=vmem,
        scratch_shapes=[pltpu.VMEM((rank, rank), jnp.float32)] if scratch else [],
        compiler_params=params(),
        cost_estimate=cost(microseconds),
        name=name,
    )(*args)


def whiten_kernel(z_ref, factor_ref, near_ref, far_ref, out_ref, core_ref, *, bits_c):
    relations, rank = out_ref.shape[0], out_ref.shape[1]
    halves = near_ref.shape[0]
    pieces = 2 * halves // relations
    height = near_ref.shape[2]
    my_col = lax.axis_index("cols")
    my_row = lax.axis_index("rows")
    core_ref[:halves] = near_ref[...]
    core_ref[halves:] = far_ref[...]
    high, low = split(lower_of(z_ref[...]), 2)
    left = jnp.concatenate([high, high, low], axis=1)
    right = jnp.concatenate([high, low, high], axis=1)
    for k in range(relations):
        parts = []
        for p in range(pieces):
            place = reversed_slot((k * pieces + p) ^ my_col, bits_c)
            parts += [core_ref[place, h ^ (my_row & 1)] for h in range(2)]
        core = jnp.concatenate(parts, axis=0) * factor_ref[0]
        first, rest = split(core, 2)
        middle = dot(left, jnp.concatenate([first, rest, first], axis=0))
        first, rest = split(middle, 2)
        out_ref[k] = dot(jnp.concatenate([first, first, rest], axis=1), right, ((1,), (1,)))


def whiten(z, factor, near, far, relations):
    rank = z.shape[0]
    vmem = pl.BlockSpec(memory_space=pltpu.VMEM)
    return pl.pallas_call(
        functools.partial(whiten_kernel, bits_c=bits_of("cols")),
        out_shape=jax.ShapeDtypeStruct((relations, rank, rank), jnp.float32),
        in_specs=[vmem, pl.BlockSpec(memory_space=pltpu.SMEM), vmem, vmem],
        out_specs=vmem,
        scratch_shapes=[pltpu.VMEM((2 * near.shape[0],) + near.shape[1:], jnp.float32)],
        compiler_params=params(),
        cost_estimate=cost(2.3),
        name="whiten",
    )(z, factor.reshape(1), near, far)


def pair_of_sums(x):
    for b in range(bits_of("cols") - 1):
        x = x + swap(x, "cols", 1 << b)
    return x, swap(x, "cols", 1 << (bits_of("cols") - 1))


def local(factor, cores, tile_values, tile_rows, tile_cols, tile_counts):
    relations, slots, tile, _ = tile_values.shape
    rank = factor.shape[1]
    n_rows, n_cols = lax.axis_size("rows"), lax.axis_size("cols")
    half = n_rows // 2
    places, scale, tiles, cores, own = prepare(
        tile_rows, tile_cols, tile_counts, tile_values, cores, factor
    )
    scale = scale[0, 0]

    factors, gram = gram_of([own] + gather_rows(factor)[1:])
    panel = gather_cols(factor)
    gram_pair = pair_of_sums(gram)
    direct, back = first_pass(places, tiles, after(factors, gram_pair[0]), panel, cores)
    direct, back = after((direct, back), gram_pair)
    system = square_call(system_kernel, "system", 5.5, rank, *gram_pair, cores)
    parts = []
    for begin in range(half, 0, -half // 2):
        begin = begin - half // 2
        end = begin + half // 2
        give = half_of(back[half + begin:half + end], scale)
        parts = [back[begin:end] + swap(give, "rows", 1).astype(jnp.float32) / scale] + parts
    packed = [after(half_of(part, scale), system) for part in parts]
    received = [
        swap(packed[i // (half // 2)][i % (half // 2)], "rows", 2 * i).astype(jnp.float32)
        for i in range(1, half)
    ]
    numerator = (
        scatter_cols(direct, scale)[0] + parts[0][0] + functools.reduce(jnp.add, received) / scale
    )
    inverse = square_call(inverse_kernel, "inverse", 4.0, rank, system, scratch=True)
    factor_new = dot(numerator, inverse, precision=lax.Precision.HIGHEST).astype(jnp.bfloat16)

    factors_new, gram_new = gram_of(gather_rows(factor_new))
    panel_new = gather_cols(factor_new)
    gram_pair = pair_of_sums(gram_new)
    core = second_pass(places, tiles, factors_new, panel_new)
    keep, give = jnp.split(after(core, gram_pair[0]), 2, axis=0)
    core = keep + swap(give, "cols", 1)
    z = square_call(begin_kernel, "begin", 3.3, rank, *gram_pair)
    bits = bits_of("cols")
    slots_left = [2 * reversed_slot(p, bits - 1) for p in range(n_cols // 2)]
    plane = [(h, p) for p in range(n_cols // 2) for h in range(2) if (h, p) != (0, 0)]
    core = core[0, 0] + functools.reduce(
        jnp.add, [swap_both(core[p, h], h, slots_left[p]) for h, p in plane]
    )
    longest = jnp.max(gram_pair[0] + gram_pair[1])
    tiles_in_all = n_rows * n_cols
    scale_core = f16_top / (2.0 * slots * tile * value_bound * tiles_in_all * longest + 1e-30)
    packed = after(half_of(core, scale_core), z)
    core = tree_sum(
        [packed.astype(jnp.float32)]
        + [swap(packed, "rows", 2 * i).astype(jnp.float32) for i in range(1, half)]
    )
    z = square_call(end_kernel, "end", 2.9, rank, z)
    core = after(core.astype(jnp.float16), z)
    found = {(h, p): swap_both(core, h, slots_left[p]) for h, p in plane}
    found[(0, 0)] = core
    near = jnp.stack(
        [jnp.stack([found[(h, p)] for h in range(2)]) for p in range(n_cols // 2)]
    )
    far = swap(near, "cols", 1)
    cores_new = whiten(
        z, 1.0 / scale_core, near.astype(jnp.float32), far.astype(jnp.float32), relations
    )
    return (factor_new, cores_new)


def solution(mesh):
    in_specs = (
        P(("rows", "cols"), None),
        P(),
        P(None, "rows", "cols", None),
        P(None, "rows", "cols"),
        P(None, "rows", "cols"),
        P(None, "rows", "cols"),
    )
    out_specs = (P(("rows", "cols"), None), P())
    return jax.shard_map(local, mesh=mesh, in_specs=in_specs, out_specs=out_specs, check_vma=False)
```

```python
import functools

import jax
import jax.numpy as jnp
from jax import lax
from jax.experimental import pallas as pl
from jax.experimental.pallas import tpu as pltpu
from jax.sharding import PartitionSpec as P

ridge_weight = 0.1
value_bound = 160.0
product_bound = 672.0
f16_top = 30000.0


def params():
    return pltpu.CompilerParams(vmem_limit_bytes=48 * 1024 * 1024)


def swap(x, axis, mask):
    size = lax.axis_size(axis)
    return lax.ppermute(x, axis, [(i, i ^ mask) for i in range(size)])


def swap_both(x, row_mask, col_mask):
    if col_mask == 0:
        return swap(x, "rows", row_mask)
    if row_mask == 0:
        return swap(x, "cols", col_mask)
    n_cols = lax.axis_size("cols")
    mask = row_mask * n_cols + col_mask
    size = lax.axis_size("rows") * n_cols
    return lax.ppermute(x, ("rows", "cols"), [(i, i ^ mask) for i in range(size)])


def cost(microseconds):
    return pl.CostEstimate(
        flops=int(microseconds * 1.1e9), bytes_accessed=100_000, transcendentals=0
    )


def after(x, other):
    return lax.optimization_barrier((x, other))[0]


def bits_of(axis):
    return lax.axis_size(axis).bit_length() - 1


def reversed_slot(slot, bits):
    out = 0
    for b in range(bits):
        out = out + (((slot >> b) & 1) << (bits - 1 - b))
    return out


def gather_cols(x):
    for b in range(bits_of("cols")):
        x = jnp.concatenate([x, swap(x, "cols", 1 << b)], axis=0)
    return x


def gather_rows(x, first=None):
    half = lax.axis_size("rows") // 2
    even = [swap(x, "rows", 2 * i) for i in range(1, half)]
    across = swap(x, "rows", 1)
    if first is not None:
        even = after(even, first)
    return [x] + even + [across] + [swap(p, "rows", 1) for p in even]


def tree_sum(parts):
    while len(parts) > 1:
        parts = [parts[i] + parts[i + 1] for i in range(0, len(parts), 2)]
    return parts[0]


def scatter_cols(x):
    for b in range(bits_of("cols")):
        keep, give = jnp.split(x, 2, axis=0)
        if b == 0:
            x = keep + swap(give, "cols", 1)
        else:
            x = keep + swap(give.astype(jnp.float16), "cols", 1 << b).astype(jnp.float32)
    return x


def dot(a, b, dims=((1,), (0,)), precision=None):
    return lax.dot_general(
        a, b, (dims, ((), ())), preferred_element_type=jnp.float32, precision=precision
    )


def gram_kernel(*refs):
    pieces, factors_ref, gram_ref = refs[:-2], refs[-2], refs[-1]
    begin = 0
    for piece in pieces:
        factors_ref[begin:begin + piece.shape[0], :] = piece[...]
        begin += piece.shape[0]
    whole = factors_ref[...]
    gram = dot(whole, whole, ((0,), (0,)))
    side = gram_ref.shape[1]
    gram_ref[0] = gram[:side, :side]
    gram_ref[1] = gram[:side, side:]
    gram_ref[2] = gram[side:, side:]


def gram_of(pieces):
    rank = pieces[0].shape[1]
    height = sum(piece.shape[0] for piece in pieces)
    vmem = pl.BlockSpec(memory_space=pltpu.VMEM)
    factors, gram = pl.pallas_call(
        gram_kernel,
        out_shape=(
            jax.ShapeDtypeStruct((height, rank), jnp.bfloat16),
            jax.ShapeDtypeStruct((3, rank // 2, rank // 2), jnp.float32),
        ),
        in_specs=[vmem] * len(pieces),
        out_specs=(vmem, vmem),
        compiler_params=params(),
        cost_estimate=cost(0.4),
        name="gram",
    )(*pieces)
    return factors, gram


def prepare_kernel(rows_hbm, cols_hbm, counts_ref, tiles_hbm, cores_hbm, factor_hbm,
                   places_ref, scale_ref, tiles_ref, copied_ref, own_ref,
                   rows_ref, cols_ref, sems, *, half, terms):
    relations, slots = tiles_ref.shape[0], tiles_ref.shape[1]
    my_row = lax.axis_index("rows")
    my_col = lax.axis_index("cols")
    copies = [
        pltpu.make_async_copy(source, target, sems.at[i])
        for i, (source, target) in enumerate(
            (
                (cores_hbm, copied_ref),
                (rows_hbm, rows_ref),
                (cols_hbm, cols_ref),
                (tiles_hbm, tiles_ref),
                (factor_hbm, own_ref),
            )
        )
    ]
    for copy in copies:
        copy.start()
    copies[0].wait()
    reach = jnp.zeros((1, 1), jnp.float32)
    for k in range(relations):
        size = jnp.abs(copied_ref[k].astype(jnp.float32))
        for axis in (0, 1):
            sums = jnp.sum(size, axis=axis, keepdims=True)
            reach = jnp.maximum(reach, jnp.max(sums, axis=1 - axis, keepdims=True))
    scale_ref[...] = jnp.broadcast_to(
        f16_top / (terms * relations * slots * product_bound * reach + 1e-20), scale_ref.shape
    )
    for copy in copies[1:]:
        copy.wait()
    for k in range(relations):
        for s in range(slots):
            col = cols_ref[k, 0, s] ^ my_row
            places_ref[k, s] = (col & 1) * half + (col >> 1)
            places_ref[k, slots + s] = rows_ref[k, 0, s] ^ my_col

            @pl.when(s >= counts_ref[k, 0, 0])
            def _():
                tiles_ref[k, s] = jnp.zeros(tiles_ref.shape[2:], tiles_ref.dtype)


def stay(x):
    return pltpu.with_memory_space_constraint(x, pltpu.HBM)


def prepare(rows, cols, counts, tiles, cores, factor):
    n_rows, n_cols = lax.axis_size("rows"), lax.axis_size("cols")
    smem = pl.BlockSpec(memory_space=pltpu.SMEM)
    vmem = pl.BlockSpec(memory_space=pltpu.VMEM)
    anywhere = pl.BlockSpec(memory_space=pltpu.HBM)
    return pl.pallas_call(
        functools.partial(prepare_kernel, half=n_rows // 2, terms=2.0 * n_cols),
        out_shape=(
            jax.ShapeDtypeStruct((tiles.shape[0], 2 * tiles.shape[1]), jnp.int32),
            jax.ShapeDtypeStruct((1, cores.shape[-1]), jnp.float32),
            jax.ShapeDtypeStruct(tiles.shape, tiles.dtype),
            jax.ShapeDtypeStruct(cores.shape, cores.dtype),
            jax.ShapeDtypeStruct(factor.shape, factor.dtype),
        ),
        in_specs=[anywhere, anywhere, smem, anywhere, anywhere, anywhere],
        out_specs=(smem, vmem, vmem, vmem, vmem),
        scratch_shapes=[
            pltpu.SMEM(rows.shape, jnp.int32),
            pltpu.SMEM(cols.shape, jnp.int32),
            pltpu.SemaphoreType.DMA((5,)),
        ],
        compiler_params=params(),
        cost_estimate=cost(2.0),
        name="prepare",
    )(
        stay(rows), stay(cols), counts, stay(tiles), stay(cores), stay(factor)
    )


def first_kernel(places_ref, scale_ref, tiles_ref, factors_ref, panel_ref, cores_ref,
                 direct_ref, back_ref, acc_ref, turned_ref, sums_ref, *, bits_c):
    relations, slots = tiles_ref.shape[0], tiles_ref.shape[1]
    tile = tiles_ref.shape[2]
    panels = panel_ref.shape[0] // tile
    sums_ref[...] = jnp.zeros_like(sums_ref)
    for k in range(relations):
        core = cores_ref[k]
        for i in range(panels):
            rotated = dot(panel_ref[i * tile:(i + 1) * tile, :], core).astype(jnp.bfloat16)
            turned_ref[i] = rotated.T
        acc_ref[...] = jnp.zeros_like(acc_ref)
        for s in range(slots):
            values = tiles_ref[k, s]
            col = places_ref[k, s]
            row = places_ref[k, slots + s]
            acc_ref[row] += dot(values, factors_ref[col])
            sums_ref[col] += dot(turned_ref[row], values)
        for i in range(panels):
            whole = acc_ref[i]
            high = whole.astype(jnp.bfloat16)
            low = (whole - high.astype(jnp.float32)).astype(jnp.bfloat16)
            part = dot(high, core, ((1,), (1,))) + dot(low, core, ((1,), (1,)))
            part = part * scale_ref[...]
            place = reversed_slot(i, bits_c)
            if k == 0:
                direct_ref[place] = part
            else:
                direct_ref[place] += part
    for g in range(sums_ref.shape[0]):
        back_ref[g] = sums_ref[g].T * scale_ref[...]


def first_pass(places, scale, tiles, factors, panel, cores):
    tile = tiles.shape[2]
    rank = cores.shape[-1]
    n_rows, n_cols = lax.axis_size("rows"), lax.axis_size("cols")
    smem = pl.BlockSpec(memory_space=pltpu.SMEM)
    vmem = pl.BlockSpec(memory_space=pltpu.VMEM)
    return pl.pallas_call(
        functools.partial(first_kernel, bits_c=bits_of("cols")),
        out_shape=(
            jax.ShapeDtypeStruct((n_cols, tile, rank), jnp.float32),
            jax.ShapeDtypeStruct((n_rows, tile, rank), jnp.float32),
        ),
        in_specs=[smem, vmem, vmem, vmem, vmem, vmem],
        out_specs=(vmem, vmem),
        scratch_shapes=[
            pltpu.VMEM((n_cols, tile, rank), jnp.float32),
            pltpu.VMEM((n_cols, rank, tile), jnp.bfloat16),
            pltpu.VMEM((n_rows, rank, tile), jnp.float32),
        ],
        compiler_params=params(),
        cost_estimate=cost(4.8),
        name="first_pass",
    )(places, scale, tiles, factors.reshape(n_rows, tile, rank), panel, cores)


def second_kernel(places_ref, tiles_ref, factors_ref, panel_ref,
                  out_ref, turned_ref, upper_ref, picked_ref, *, bits_c):
    relations, slots = tiles_ref.shape[0], tiles_ref.shape[1]
    tile = tiles_ref.shape[2]
    panels = panel_ref.shape[0] // tile
    pieces = out_ref.shape[0] // relations
    height = out_ref.shape[2]
    my_row = lax.axis_index("rows")
    my_col = lax.axis_index("cols")
    for i in range(panels):
        turned_ref[i] = panel_ref[i * tile:(i + 1) * tile, :].T
    for k in range(relations):
        for s in range(slots):
            values = tiles_ref[k, s]
            col = places_ref[k, s]
            row = places_ref[k, slots + s]
            upper_ref[:, s * tile:(s + 1) * tile] = dot(turned_ref[row], values).astype(jnp.bfloat16)
            picked_ref[s * tile:(s + 1) * tile, :] = factors_ref[col]
        core = dot(upper_ref[...], picked_ref[...])
        for p in range(pieces):
            place = reversed_slot((k * pieces + p) ^ my_col, bits_c)
            for h in range(2):
                begin = (2 * p + h) * height
                out_ref[place, h ^ (my_row & 1)] = core[begin:begin + height, :]


def second_pass(places, tiles, factors, panel):
    relations, slots, tile, _ = tiles.shape
    rank = panel.shape[-1]
    n_rows, n_cols = lax.axis_size("rows"), lax.axis_size("cols")
    smem = pl.BlockSpec(memory_space=pltpu.SMEM)
    vmem = pl.BlockSpec(memory_space=pltpu.VMEM)
    return pl.pallas_call(
        functools.partial(second_kernel, bits_c=bits_of("cols")),
        out_shape=jax.ShapeDtypeStruct(
            (n_cols, 2, relations * rank // n_cols // 2, rank), jnp.float32
        ),
        in_specs=[smem, vmem, vmem, vmem],
        out_specs=vmem,
        scratch_shapes=[
            pltpu.VMEM((n_cols, rank, tile), jnp.bfloat16),
            pltpu.VMEM((rank, slots * tile), jnp.bfloat16),
            pltpu.VMEM((slots * tile, rank), jnp.bfloat16),
        ],
        compiler_params=params(),
        cost_estimate=cost(2.8),
        name="second_pass",
    )(places, tiles, factors.reshape(n_rows, tile, rank), panel)


def split(x, terms):
    parts = []
    for _ in range(terms):
        part = x.astype(jnp.bfloat16)
        parts.append(part)
        x = x - part.astype(jnp.float32)
    return parts


def eliminate(z_ref, begin, end, block, sub):
    size = z_ref.shape[0]
    wide = size // 128
    groups = block // 8
    rows = lax.broadcasted_iota(jnp.int32, (8, 128), 0)
    rows_wide = lax.broadcasted_iota(jnp.int32, (8, size), 0)
    lanes = lax.broadcasted_iota(jnp.int32, (8, size), 1)
    for p in range(begin, end):
        o = p * block
        panel = [z_ref[o + 8 * g:o + 8 * g + 8, :] for g in range(groups)]
        for q in range(block // sub):
            first = o + q * sub
            start = q * sub // 8
            cols = [
                {
                    g: jnp.broadcast_to(panel[g][:, first + m:first + m + 1], (8, 128))
                    for g in range(start, groups)
                }
                for m in range(sub)
            ]
            for m in range(sub):
                j = q * sub + m
                own, i = j // 8, j % 8
                root = lax.rsqrt(cols[m][own][i:i + 1, :])
                factors = {g: cols[m][g] * root for g in range(own, groups)}
                factors[own] = jnp.where(rows > i, factors[own], 0.0)
                for t in range(m + 1, sub):
                    line = cols[t][own][i:i + 1, :] * root
                    for g in range(own, groups):
                        cols[t][g] = cols[t][g] - factors[g] * line
                pivot = lanes == o + j
                panel[own] = jnp.where(pivot, jnp.where(rows_wide == i, 1.0, 0.0), panel[own])
                line = panel[own][i:i + 1, :] * jnp.concatenate([root] * wide, axis=1)
                for g in range(own, groups):
                    factor = jnp.concatenate([factors[g]] * wide, axis=1)
                    if g > own:
                        panel[g] = jnp.where(pivot, 0.0, panel[g])
                    panel[g] = panel[g] - factor * line
                panel[own] = jnp.where(rows_wide == i, line, panel[own])
        panel = jnp.concatenate(panel, axis=0)
        below = lax.broadcasted_iota(jnp.int32, (block, size), 0) + o
        across = lax.broadcasted_iota(jnp.int32, (block, size), 1)
        panel = jnp.where((across > below) & (across < o + block), 0.0, panel)
        z_ref[o:o + block, :] = panel
        rest = size - o - block
        if rest:
            high, mid, low = split(panel, 3)
            left = jnp.concatenate([high, high, mid, mid, high, low], axis=0)[:, o + block:]
            right = jnp.concatenate([high, mid, high, mid, low, high], axis=0)
            change = dot(left, right, ((0,), (0,)))
            spread = lax.broadcasted_iota(jnp.int32, (rest, size), 1)
            done = (spread >= o) & (spread < o + block)
            z_ref[o + block:, :] = jnp.where(done, 0.0, z_ref[o + block:, :]) - change


def lower_of(z):
    rows = lax.broadcasted_iota(jnp.int32, z.shape, 0)
    lanes = lax.broadcasted_iota(jnp.int32, z.shape, 1)
    return jnp.where(rows >= lanes, z, 0.0)


def system_kernel(mine_ref, other_ref, cores_ref, z_ref):
    size = z_ref.shape[0]
    side = size // 2
    upper = mine_ref[1] + other_ref[1]
    z_ref[:side, :side] = mine_ref[0] + other_ref[0]
    z_ref[:side, side:] = upper
    z_ref[side:, :side] = upper.T
    z_ref[side:, side:] = mine_ref[2] + other_ref[2]
    grams = jnp.concatenate(split(z_ref[...], 3), axis=0)
    rows = lax.broadcasted_iota(jnp.int32, (size, size), 0)
    lanes = lax.broadcasted_iota(jnp.int32, (size, size), 1)
    total = jnp.where(rows == lanes, ridge_weight, 0.0)
    for k in range(cores_ref.shape[0]):
        core = cores_ref[k]
        turned = core.T
        for left, right in ((core, turned), (turned, core)):
            middle = dot(jnp.concatenate([left] * 3, axis=1), grams)
            middle = jnp.concatenate(split(middle, 3), axis=1)
            total = total + dot(middle, jnp.concatenate([right] * 3, axis=0))
    z_ref[...] = total
    eliminate(z_ref, 0, 3 * size // 256, 32, 16)


def inverse_kernel(in_ref, scale_ref, out_ref, z_ref):
    size = z_ref.shape[0]
    z_ref[...] = in_ref[...]
    eliminate(z_ref, 3 * size // 256, size // 32, 32, 16)
    high, mid, low = split(lower_of(z_ref[...]), 3)
    left = jnp.concatenate([high, high, mid, mid, high, low], axis=0)
    right = jnp.concatenate([high, mid, high, mid, low, high], axis=0)
    out_ref[...] = dot(left, right, ((0,), (0,))) / scale_ref[...]


def scale_kernel(mine_ref, other_ref, scale_ref, back_ref, *, bound):
    largest = jnp.max(mine_ref[...] + other_ref[...], axis=0)
    largest = jnp.max(jnp.max(largest, axis=0, keepdims=True), axis=1, keepdims=True)
    scale = f16_top / (bound * jnp.broadcast_to(largest, scale_ref.shape) + 1e-30)
    scale_ref[...] = scale
    back_ref[...] = 1.0 / scale


def core_scale(pair, rank, bound):
    vmem = pl.BlockSpec(memory_space=pltpu.VMEM)
    vector = jax.ShapeDtypeStruct((1, rank), jnp.float32)
    return pl.pallas_call(
        functools.partial(scale_kernel, bound=bound),
        out_shape=(vector, vector),
        in_specs=[vmem, vmem],
        out_specs=(vmem, vmem),
        compiler_params=params(),
        cost_estimate=cost(0.5),
        name="core_scale",
    )(*pair)


def begin_kernel(mine_ref, other_ref, out_ref):
    size = out_ref.shape[0]
    side = size // 2
    out_ref[:side, :side] = mine_ref[0] + other_ref[0]
    out_ref[:side, side:] = mine_ref[1] + other_ref[1]
    out_ref[side:, :side] = jnp.zeros((side, side), jnp.float32)
    out_ref[side:, side:] = mine_ref[2] + other_ref[2]
    eliminate(out_ref, 0, size // 64, 32, 16)


def end_kernel(in_ref, out_ref):
    size = out_ref.shape[0]
    out_ref[...] = in_ref[...]
    eliminate(out_ref, size // 64, size // 32, 32, 16)


def square_call(kernel, name, microseconds, rank, *args, scratch=False):
    vmem = pl.BlockSpec(memory_space=pltpu.VMEM)
    return pl.pallas_call(
        kernel,
        out_shape=jax.ShapeDtypeStruct((rank, rank), jnp.float32),
        in_specs=[vmem] * len(args),
        out_specs=vmem,
        scratch_shapes=[pltpu.VMEM((rank, rank), jnp.float32)] if scratch else [],
        compiler_params=params(),
        cost_estimate=cost(microseconds),
        name=name,
    )(*args)


def whitened(left, right, core):
    first, rest = split(core, 2)
    middle = dot(left, jnp.concatenate([first, rest, first], axis=0))
    first, rest = split(middle, 2)
    return dot(jnp.concatenate([first, first, rest], axis=1), right, ((1,), (1,)))


def whiten_parts(z_ref):
    high, low = split(lower_of(z_ref[...]), 2)
    left = jnp.concatenate([high, high, low], axis=1)
    right = jnp.concatenate([high, low, high], axis=1)
    return left, right


def whiten_kernel(z_ref, factor_ref, near_ref, far_ref, out_ref, core_ref, *, bits_c):
    relations, halves = out_ref.shape[0], near_ref.shape[0]
    pieces = 2 * halves // relations
    my_col = lax.axis_index("cols")
    my_row = lax.axis_index("rows")
    left, right = whiten_parts(z_ref)
    core_ref[:halves] = near_ref[...]
    core_ref[halves:] = far_ref[...]
    for k in range(relations):
        parts = []
        for p in range(pieces):
            place = reversed_slot((k * pieces + p) ^ my_col, bits_c)
            parts += [core_ref[place, h ^ (my_row & 1)] for h in range(2)]
        core = jnp.concatenate(parts, axis=0) * factor_ref[...]
        out_ref[k] = whitened(left, right, core)


def half_whiten_kernel(z_ref, factor_ref, core_ref, *refs, bits_c):
    out_ref = refs[-1]
    my_col = lax.axis_index("cols")
    my_row = lax.axis_index("rows")
    left, right = whiten_parts(z_ref)
    for p in range(core_ref.shape[0]):
        slot = 2 * reversed_slot(p, bits_c - 1)
        parts = [core_ref[p, h ^ (my_row & 1)] for h in range(2)]
        core = jnp.concatenate(parts, axis=0) * factor_ref[...]
        result = whitened(left, right, core)
        if len(refs) == 1:
            out_ref[p] = result
        else:
            out_ref[slot ^ my_col] = refs[0][p]
            out_ref[(slot + 1) ^ my_col] = result


def whiten(z, factor, near, far, relations):
    rank = z.shape[0]
    halves = near.shape[0]
    vmem = pl.BlockSpec(memory_space=pltpu.VMEM)

    def call(kernel, count, microseconds, *args, scratch=()):
        return pl.pallas_call(
            functools.partial(kernel, bits_c=bits_of("cols")),
            out_shape=jax.ShapeDtypeStruct((count, rank, rank), jnp.float32),
            in_specs=[vmem] * (2 + len(args)),
            out_specs=vmem,
            scratch_shapes=scratch,
            compiler_params=params(),
            cost_estimate=cost(microseconds),
            name="whiten",
        )(z, factor, *args)

    if 2 * halves != relations:
        scratch = [pltpu.VMEM((2 * halves,) + near.shape[1:], jnp.float32)]
        return call(whiten_kernel, relations, 2.3, near, far, scratch=scratch)
    first = call(half_whiten_kernel, halves, 1.2, near)
    return call(half_whiten_kernel, relations, 1.2, far, first)


def pair_of_sums(x):
    for b in range(bits_of("cols") - 1):
        x = x + swap(x, "cols", 1 << b)
    return x, swap(x, "cols", 1 << (bits_of("cols") - 1))


def local(factor, cores, tile_values, tile_rows, tile_cols, tile_counts):
    relations, slots, tile, _ = tile_values.shape
    rank = factor.shape[1]
    n_rows, n_cols = lax.axis_size("rows"), lax.axis_size("cols")
    half = n_rows // 2
    places, scale, tiles, cores, own = prepare(
        tile_rows, tile_cols, tile_counts, tile_values, cores, factor
    )

    factors, gram = gram_of([own] + gather_rows(factor, own)[1:])
    panel = gather_cols(factor)
    gram_pair = pair_of_sums(gram)
    direct, back = first_pass(places, scale, tiles, after(factors, gram_pair[0]), panel, cores)
    direct, back = after((direct, back), gram_pair)
    system = square_call(system_kernel, "system", 3.8, rank, *gram_pair, cores)
    middle = half + half // 2
    far = swap(back[middle:].astype(jnp.float16), "rows", 1).astype(jnp.float32)
    close = swap(back[half:middle].astype(jnp.float16), "rows", 1).astype(jnp.float32)
    far = back[half // 2:half] + far
    close = back[:half // 2] + close
    packed = [
        after(x[i].astype(jnp.float16), system) for x in (close, far) for i in range(half // 2)
    ]
    packed[half - 1] = after(packed[half - 1], close)
    received = [swap(packed[i], "rows", 2 * i).astype(jnp.float32) for i in range(1, half)]
    numerator = scatter_cols(direct)[0] + close[0] + functools.reduce(jnp.add, received)
    inverse = square_call(inverse_kernel, "inverse", 5.2, rank, system, scale, scratch=True)
    factor_new = dot(numerator, inverse, precision=lax.Precision.HIGHEST).astype(jnp.bfloat16)

    factors_new, gram_new = gram_of(gather_rows(factor_new))
    panel_new = gather_cols(factor_new)
    gram_pair = pair_of_sums(gram_new)
    core = second_pass(places, tiles, factors_new, panel_new)
    keep, give = jnp.split(after(core, gram_pair[0]), 2, axis=0)
    core = keep + swap(give, "cols", 1)
    bits = bits_of("cols")
    slots_left = [2 * reversed_slot(p, bits - 1) for p in range(n_cols // 2)]
    plane = [(h, p) for p in range(n_cols // 2) for h in range(2) if (h, p) != (0, 0)]
    core = core[0, 0] + functools.reduce(
        jnp.add, [swap_both(core[p, h], h, slots_left[p]) for h, p in plane]
    )
    bound = 2.0 * slots * tile * value_bound * n_rows * n_cols
    scale_core, unit_core = core_scale(gram_pair, rank, bound)
    z = square_call(begin_kernel, "begin", 3.3, rank, *gram_pair)
    packed = (core * scale_core).astype(jnp.float16)
    core = tree_sum(
        [packed.astype(jnp.float32)]
        + [swap(packed, "rows", 2 * i).astype(jnp.float32) for i in range(1, half)]
    )
    core = after(core.astype(jnp.float16), z)
    found = {(h, p): swap_both(core, h, slots_left[p]) for h, p in plane}
    z = square_call(end_kernel, "end", 2.9, rank, after(z, found[plane[0]]))
    found[(0, 0)] = core
    near = jnp.stack(
        [jnp.stack([found[(h, p)] for h in range(2)]) for p in range(n_cols // 2)]
    )
    near = after(near, z)
    far = swap(near, "cols", 1)
    cores_new = whiten(
        z, unit_core, near.astype(jnp.float32), far.astype(jnp.float32), relations
    )
    return (factor_new, cores_new)


def solution(mesh):
    in_specs = (
        P(("rows", "cols"), None),
        P(),
        P(None, "rows", "cols", None),
        P(None, "rows", "cols"),
        P(None, "rows", "cols"),
        P(None, "rows", "cols"),
    )
    out_specs = (P(("rows", "cols"), None), P())
    return jax.shard_map(local, mesh=mesh, in_specs=in_specs, out_specs=out_specs, check_vma=False)
```

```python
import functools

import jax
import jax.numpy as jnp
from jax import lax
from jax.experimental import pallas as pl
from jax.experimental.pallas import tpu as pltpu
from jax.sharding import PartitionSpec as P

ridge_weight = 0.1
product_bound = 672.0
f16_top = 30000.0
extra_rows = 16


def params():
    return pltpu.CompilerParams(vmem_limit_bytes=48 * 1024 * 1024)


def swap(x, axis, mask):
    size = lax.axis_size(axis)
    return lax.ppermute(x, axis, [(i, i ^ mask) for i in range(size)])


def swap_both(x, row_mask, col_mask):
    if col_mask == 0:
        return swap(x, "rows", row_mask)
    if row_mask == 0:
        return swap(x, "cols", col_mask)
    n_cols = lax.axis_size("cols")
    mask = row_mask * n_cols + col_mask
    size = lax.axis_size("rows") * n_cols
    return lax.ppermute(x, ("rows", "cols"), [(i, i ^ mask) for i in range(size)])


def cost(microseconds):
    return pl.CostEstimate(
        flops=int(microseconds * 1.1e9), bytes_accessed=100_000, transcendentals=0
    )


def after(x, other):
    return lax.optimization_barrier((x, other))[0]


def bits_of(axis):
    return lax.axis_size(axis).bit_length() - 1


def reversed_slot(slot, bits):
    out = 0
    for b in range(bits):
        out = out + (((slot >> b) & 1) << (bits - 1 - b))
    return out


def gather_cols(x):
    for b in range(bits_of("cols")):
        x = jnp.concatenate([x, swap(x, "cols", 1 << b)], axis=0)
    return x


def gather_rows(x, first=None):
    half = lax.axis_size("rows") // 2
    even = [swap(x, "rows", 2 * i) for i in range(1, half)]
    across = swap(x, "rows", 1)
    if first is not None:
        even = after(even, first)
    return [x] + even + [across] + [swap(p, "rows", 1) for p in even]


def tree_sum(parts):
    while len(parts) > 1:
        parts = [parts[i] + parts[i + 1] for i in range(0, len(parts), 2)]
    return parts[0]


def scatter_cols(x):
    for b in range(bits_of("cols")):
        keep, give = jnp.split(x, 2, axis=0)
        if b == 0:
            x = keep + swap(give, "cols", 1)
        else:
            x = keep + swap(give.astype(jnp.float16), "cols", 1 << b).astype(jnp.float32)
    return x


def dot(a, b, dims=((1,), (0,)), precision=None):
    return lax.dot_general(
        a, b, (dims, ((), ())), preferred_element_type=jnp.float32, precision=precision
    )


def gram_kernel(*refs):
    pieces, factors_ref, gram_ref = refs[:-2], refs[-2], refs[-1]
    begin = 0
    for piece in pieces:
        factors_ref[begin:begin + piece.shape[0], :] = piece[...]
        begin += piece.shape[0]
    whole = factors_ref[...]
    gram = dot(whole, whole, ((0,), (0,)))
    side = gram_ref.shape[1]
    gram_ref[0] = gram[:side, :side]
    gram_ref[1] = gram[:side, side:]
    gram_ref[2] = gram[side:, side:]


def gram_of(pieces):
    rank = pieces[0].shape[1]
    height = sum(piece.shape[0] for piece in pieces)
    vmem = pl.BlockSpec(memory_space=pltpu.VMEM)
    factors, gram = pl.pallas_call(
        gram_kernel,
        out_shape=(
            jax.ShapeDtypeStruct((height, rank), jnp.bfloat16),
            jax.ShapeDtypeStruct((3, rank // 2, rank // 2), jnp.float32),
        ),
        in_specs=[vmem] * len(pieces),
        out_specs=(vmem, vmem),
        compiler_params=params(),
        cost_estimate=cost(0.4),
        name="gram",
    )(*pieces)
    return factors, gram


def prepare_kernel(rows_hbm, cols_hbm, counts_ref, tiles_hbm, cores_hbm, factor_hbm,
                   places_ref, scale_ref, tiles_ref, copied_ref, own_ref,
                   rows_ref, cols_ref, sems, *, half, terms):
    relations, slots = tiles_ref.shape[0], tiles_ref.shape[1]
    my_row = lax.axis_index("rows")
    my_col = lax.axis_index("cols")
    copies = [
        pltpu.make_async_copy(source, target, sems.at[i])
        for i, (source, target) in enumerate(
            (
                (cores_hbm, copied_ref),
                (rows_hbm, rows_ref),
                (cols_hbm, cols_ref),
                (tiles_hbm, tiles_ref),
                (factor_hbm, own_ref),
            )
        )
    ]
    for copy in copies:
        copy.start()
    copies[0].wait()
    reach = jnp.zeros((1, 1), jnp.float32)
    for k in range(relations):
        size = jnp.abs(copied_ref[k].astype(jnp.float32))
        for axis in (0, 1):
            sums = jnp.sum(size, axis=axis, keepdims=True)
            reach = jnp.maximum(reach, jnp.max(sums, axis=1 - axis, keepdims=True))
    scale_ref[...] = jnp.broadcast_to(
        f16_top / (terms * relations * slots * product_bound * reach + 1e-20), scale_ref.shape
    )
    for copy in copies[1:]:
        copy.wait()
    for k in range(relations):
        for s in range(slots):
            col = cols_ref[k, 0, s] ^ my_row
            places_ref[k, s] = (col & 1) * half + (col >> 1)
            places_ref[k, slots + s] = rows_ref[k, 0, s] ^ my_col

            @pl.when(s >= counts_ref[k, 0, 0])
            def _():
                tiles_ref[k, s] = jnp.zeros(tiles_ref.shape[2:], tiles_ref.dtype)


def stay(x):
    return pltpu.with_memory_space_constraint(x, pltpu.HBM)


def prepare(rows, cols, counts, tiles, cores, factor):
    n_rows, n_cols = lax.axis_size("rows"), lax.axis_size("cols")
    smem = pl.BlockSpec(memory_space=pltpu.SMEM)
    vmem = pl.BlockSpec(memory_space=pltpu.VMEM)
    anywhere = pl.BlockSpec(memory_space=pltpu.HBM)
    return pl.pallas_call(
        functools.partial(prepare_kernel, half=n_rows // 2, terms=2.0 * n_cols),
        out_shape=(
            jax.ShapeDtypeStruct((tiles.shape[0], 2 * tiles.shape[1]), jnp.int32),
            jax.ShapeDtypeStruct((1, cores.shape[-1]), jnp.float32),
            jax.ShapeDtypeStruct(tiles.shape, tiles.dtype),
            jax.ShapeDtypeStruct(cores.shape, cores.dtype),
            jax.ShapeDtypeStruct(factor.shape, factor.dtype),
        ),
        in_specs=[anywhere, anywhere, smem, anywhere, anywhere, anywhere],
        out_specs=(smem, vmem, vmem, vmem, vmem),
        scratch_shapes=[
            pltpu.SMEM(rows.shape, jnp.int32),
            pltpu.SMEM(cols.shape, jnp.int32),
            pltpu.SemaphoreType.DMA((5,)),
        ],
        compiler_params=params(),
        cost_estimate=cost(2.0),
        name="prepare",
    )(
        stay(rows), stay(cols), counts, stay(tiles), stay(cores), stay(factor)
    )


def first_kernel(places_ref, scale_ref, tiles_ref, factors_ref, panel_ref, cores_ref,
                 direct_ref, back_ref, acc_ref, turned_ref, sums_ref, *, bits_c):
    relations, slots = tiles_ref.shape[0], tiles_ref.shape[1]
    tile = tiles_ref.shape[2]
    panels = panel_ref.shape[0] // tile
    sums_ref[...] = jnp.zeros_like(sums_ref)
    for k in range(relations):
        core = cores_ref[k]
        for i in range(panels):
            rotated = dot(panel_ref[i * tile:(i + 1) * tile, :], core).astype(jnp.bfloat16)
            turned_ref[i] = rotated.T
        acc_ref[...] = jnp.zeros_like(acc_ref)
        for s in range(slots):
            values = tiles_ref[k, s]
            col = places_ref[k, s]
            row = places_ref[k, slots + s]
            acc_ref[row] += dot(values, factors_ref[col])
            sums_ref[col] += dot(turned_ref[row], values)
        for i in range(panels):
            whole = acc_ref[i]
            high = whole.astype(jnp.bfloat16)
            low = (whole - high.astype(jnp.float32)).astype(jnp.bfloat16)
            part = dot(high, core, ((1,), (1,))) + dot(low, core, ((1,), (1,)))
            part = part * scale_ref[...]
            place = reversed_slot(i, bits_c)
            if k == 0:
                direct_ref[place] = part
            else:
                direct_ref[place] += part
    for g in range(sums_ref.shape[0]):
        back_ref[g] = sums_ref[g].T * scale_ref[...]


def first_pass(places, scale, tiles, factors, panel, cores):
    tile = tiles.shape[2]
    rank = cores.shape[-1]
    n_rows, n_cols = lax.axis_size("rows"), lax.axis_size("cols")
    smem = pl.BlockSpec(memory_space=pltpu.SMEM)
    vmem = pl.BlockSpec(memory_space=pltpu.VMEM)
    return pl.pallas_call(
        functools.partial(first_kernel, bits_c=bits_of("cols")),
        out_shape=(
            jax.ShapeDtypeStruct((n_cols, tile, rank), jnp.float32),
            jax.ShapeDtypeStruct((n_rows, tile, rank), jnp.float32),
        ),
        in_specs=[smem, vmem, vmem, vmem, vmem, vmem],
        out_specs=(vmem, vmem),
        scratch_shapes=[
            pltpu.VMEM((n_cols, tile, rank), jnp.float32),
            pltpu.VMEM((n_cols, rank, tile), jnp.bfloat16),
            pltpu.VMEM((n_rows, rank, tile), jnp.float32),
        ],
        compiler_params=params(),
        cost_estimate=cost(4.8),
        name="first_pass",
    )(places, scale, tiles, factors.reshape(n_rows, tile, rank), panel, cores)


def second_kernel(places_ref, tiles_ref, factors_ref, panel_ref,
                  out_ref, turned_ref, upper_ref, picked_ref, *, bits_c):
    relations, slots = tiles_ref.shape[0], tiles_ref.shape[1]
    tile = tiles_ref.shape[2]
    panels = panel_ref.shape[0] // tile
    pieces = out_ref.shape[0] // relations
    height = out_ref.shape[2]
    my_row = lax.axis_index("rows")
    my_col = lax.axis_index("cols")
    for i in range(panels):
        turned_ref[i] = panel_ref[i * tile:(i + 1) * tile, :].T
    for k in range(relations):
        for s in range(slots):
            values = tiles_ref[k, s]
            col = places_ref[k, s]
            row = places_ref[k, slots + s]
            upper_ref[:, s * tile:(s + 1) * tile] = dot(turned_ref[row], values).astype(jnp.bfloat16)
            picked_ref[s * tile:(s + 1) * tile, :] = factors_ref[col]
        core = dot(upper_ref[...], picked_ref[...])
        for p in range(pieces):
            place = reversed_slot((k * pieces + p) ^ my_col, bits_c)
            for h in range(2):
                begin = (2 * p + h) * height
                out_ref[place, h ^ (my_row & 1)] = core[begin:begin + height, :]


def second_pass(places, tiles, factors, panel):
    relations, slots, tile, _ = tiles.shape
    rank = panel.shape[-1]
    n_rows, n_cols = lax.axis_size("rows"), lax.axis_size("cols")
    smem = pl.BlockSpec(memory_space=pltpu.SMEM)
    vmem = pl.BlockSpec(memory_space=pltpu.VMEM)
    return pl.pallas_call(
        functools.partial(second_kernel, bits_c=bits_of("cols")),
        out_shape=jax.ShapeDtypeStruct(
            (n_cols, 2, relations * rank // n_cols // 2, rank), jnp.float32
        ),
        in_specs=[smem, vmem, vmem, vmem],
        out_specs=vmem,
        scratch_shapes=[
            pltpu.VMEM((n_cols, rank, tile), jnp.bfloat16),
            pltpu.VMEM((rank, slots * tile), jnp.bfloat16),
            pltpu.VMEM((slots * tile, rank), jnp.bfloat16),
        ],
        compiler_params=params(),
        cost_estimate=cost(2.8),
        name="second_pass",
    )(places, tiles, factors.reshape(n_rows, tile, rank), panel)


def split(x, terms):
    parts = []
    for _ in range(terms):
        part = x.astype(jnp.bfloat16)
        parts.append(part)
        x = x - part.astype(jnp.float32)
    return parts


def eliminate(z_ref, begin, end, block, sub):
    size = z_ref.shape[0]
    wide = size // 128
    groups = block // 8
    rows = lax.broadcasted_iota(jnp.int32, (8, 128), 0)
    rows_wide = lax.broadcasted_iota(jnp.int32, (8, size), 0)
    lanes = lax.broadcasted_iota(jnp.int32, (8, size), 1)
    for p in range(begin, end):
        o = p * block
        panel = [z_ref[o + 8 * g:o + 8 * g + 8, :] for g in range(groups)]
        for q in range(block // sub):
            first = o + q * sub
            start = q * sub // 8
            cols = [
                {
                    g: jnp.broadcast_to(panel[g][:, first + m:first + m + 1], (8, 128))
                    for g in range(start, groups)
                }
                for m in range(sub)
            ]
            for m in range(sub):
                j = q * sub + m
                own, i = j // 8, j % 8
                root = lax.rsqrt(cols[m][own][i:i + 1, :])
                factors = {g: cols[m][g] * root for g in range(own, groups)}
                factors[own] = jnp.where(rows > i, factors[own], 0.0)
                for t in range(m + 1, sub):
                    line = cols[t][own][i:i + 1, :] * root
                    for g in range(own, groups):
                        cols[t][g] = cols[t][g] - factors[g] * line
                pivot = lanes == o + j
                panel[own] = jnp.where(pivot, jnp.where(rows_wide == i, 1.0, 0.0), panel[own])
                line = panel[own][i:i + 1, :] * jnp.concatenate([root] * wide, axis=1)
                for g in range(own, groups):
                    factor = jnp.concatenate([factors[g]] * wide, axis=1)
                    if g > own:
                        panel[g] = jnp.where(pivot, 0.0, panel[g])
                    panel[g] = panel[g] - factor * line
                panel[own] = jnp.where(rows_wide == i, line, panel[own])
        panel = jnp.concatenate(panel, axis=0)
        below = lax.broadcasted_iota(jnp.int32, (block, size), 0) + o
        across = lax.broadcasted_iota(jnp.int32, (block, size), 1)
        panel = jnp.where((across > below) & (across < o + block), 0.0, panel)
        z_ref[o:o + block, :] = panel
        rest = size - o - block
        if rest:
            high, mid, low = split(panel, 3)
            left = jnp.concatenate([high, high, mid, mid, high, low], axis=0)[:, o + block:]
            right = jnp.concatenate([high, mid, high, mid, low, high], axis=0)
            change = dot(left, right, ((0,), (0,)))
            spread = lax.broadcasted_iota(jnp.int32, (rest, size), 1)
            done = (spread >= o) & (spread < o + block)
            z_ref[o + block:, :] = jnp.where(done, 0.0, z_ref[o + block:, :]) - change


def lower_of(z):
    rows = lax.broadcasted_iota(jnp.int32, z.shape, 0)
    lanes = lax.broadcasted_iota(jnp.int32, z.shape, 1)
    return jnp.where(rows >= lanes, z, 0.0)


def system_kernel(mine_ref, other_ref, cores_ref, z_ref):
    size = z_ref.shape[0]
    side = size // 2
    upper = mine_ref[1] + other_ref[1]
    z_ref[:side, :side] = mine_ref[0] + other_ref[0]
    z_ref[:side, side:] = upper
    z_ref[side:, :side] = upper.T
    z_ref[side:, side:] = mine_ref[2] + other_ref[2]
    grams = jnp.concatenate(split(z_ref[...], 3), axis=0)
    rows = lax.broadcasted_iota(jnp.int32, (size, size), 0)
    lanes = lax.broadcasted_iota(jnp.int32, (size, size), 1)
    total = jnp.where(rows == lanes, ridge_weight, 0.0)
    for k in range(cores_ref.shape[0]):
        core = cores_ref[k]
        turned = core.T
        for left, right in ((core, turned), (turned, core)):
            middle = dot(jnp.concatenate([left] * 3, axis=1), grams)
            middle = jnp.concatenate(split(middle, 3), axis=1)
            total = total + dot(middle, jnp.concatenate([right] * 3, axis=0))
    z_ref[...] = total
    eliminate(z_ref, 0, 3 * size // 256, 32, 16)


def inverse_kernel(in_ref, scale_ref, out_ref, z_ref):
    size = z_ref.shape[0]
    z_ref[...] = in_ref[...]
    eliminate(z_ref, 3 * size // 256, size // 32, 32, 16)
    high, mid, low = split(lower_of(z_ref[...]), 3)
    left = jnp.concatenate([high, high, mid, mid, high, low], axis=0)
    right = jnp.concatenate([high, mid, high, mid, low, high], axis=0)
    out_ref[...] = dot(left, right, ((0,), (0,))) / scale_ref[...]


def power_of_two(exponent):
    left = jnp.abs(exponent)
    result = jnp.ones_like(exponent)
    for b in reversed(range(7)):
        taken = left >= float(1 << b)
        step = jnp.where(exponent < 0.0, 0.5 ** (1 << b), 2.0 ** (1 << b))
        result = jnp.where(taken, result * step, result)
        left = jnp.where(taken, left - float(1 << b), left)
    return result


def packed_block(x):
    top = jnp.maximum(jnp.max(jnp.abs(x), axis=0, keepdims=True), 1e-30)
    exponent = jnp.clip(jnp.ceil(jnp.log2(top)), -100.0, 126.0)
    exponents = jnp.broadcast_to(exponent, (extra_rows, x.shape[1]))
    return jnp.concatenate([x * power_of_two(-exponent), exponents], axis=0)


def unpacked_block(x):
    height = x.shape[0] - extra_rows
    return x[:height] * power_of_two(x[height:height + 1])


def plane_kernel(keep_ref, other_ref, own_ref, packed_ref):
    own_ref[...] = keep_ref[0, 0] + other_ref[0, 0]
    for i in range(packed_ref.shape[0]):
        p, h = (i + 1) // 2, (i + 1) % 2
        packed_ref[i] = packed_block(keep_ref[p, h] + other_ref[p, h])


def pack_plane(keep, other):
    pieces, _, height, rank = keep.shape
    vmem = pl.BlockSpec(memory_space=pltpu.VMEM)
    return pl.pallas_call(
        plane_kernel,
        out_shape=(
            jax.ShapeDtypeStruct((height, rank), jnp.float32),
            jax.ShapeDtypeStruct((2 * pieces - 1, height + extra_rows, rank), jnp.float32),
        ),
        in_specs=[vmem, vmem],
        out_specs=(vmem, vmem),
        compiler_params=params(),
        cost_estimate=cost(0.6),
        name="pack_plane",
    )(keep, other)


def merge_kernel(*refs, plain):
    parts = [ref[...] for ref in refs[:plain]]
    parts += [unpacked_block(ref[...]) for ref in refs[plain:-1]]
    refs[-1][...] = packed_block(tree_sum(parts))


def merge(plain, packed):
    args = list(plain) + [x.astype(jnp.float32) for x in packed]
    vmem = pl.BlockSpec(memory_space=pltpu.VMEM)
    merged = pl.pallas_call(
        functools.partial(merge_kernel, plain=len(plain)),
        out_shape=jax.ShapeDtypeStruct(args[-1].shape, jnp.float32),
        in_specs=[vmem] * len(args),
        out_specs=vmem,
        compiler_params=params(),
        cost_estimate=cost(0.5),
        name="merge",
    )(*args)
    return lax.optimization_barrier(merged.astype(jnp.float16))


def begin_kernel(mine_ref, other_ref, out_ref):
    size = out_ref.shape[0]
    side = size // 2
    out_ref[:side, :side] = mine_ref[0] + other_ref[0]
    out_ref[:side, side:] = mine_ref[1] + other_ref[1]
    out_ref[side:, :side] = jnp.zeros((side, side), jnp.float32)
    out_ref[side:, side:] = mine_ref[2] + other_ref[2]
    eliminate(out_ref, 0, size // 64, 32, 16)


def end_kernel(in_ref, out_ref):
    size = out_ref.shape[0]
    out_ref[...] = in_ref[...]
    eliminate(out_ref, size // 64, size // 32, 32, 16)


def square_call(kernel, name, microseconds, rank, *args, scratch=False):
    vmem = pl.BlockSpec(memory_space=pltpu.VMEM)
    return pl.pallas_call(
        kernel,
        out_shape=jax.ShapeDtypeStruct((rank, rank), jnp.float32),
        in_specs=[vmem] * len(args),
        out_specs=vmem,
        scratch_shapes=[pltpu.VMEM((rank, rank), jnp.float32)] if scratch else [],
        compiler_params=params(),
        cost_estimate=cost(microseconds),
        name=name,
    )(*args)


def whitened(left, right, core):
    first, rest = split(core, 2)
    middle = dot(left, jnp.concatenate([first, rest, first], axis=0))
    first, rest = split(middle, 2)
    return dot(jnp.concatenate([first, first, rest], axis=1), right, ((1,), (1,)))


def whiten_parts(z_ref):
    high, low = split(lower_of(z_ref[...]), 2)
    left = jnp.concatenate([high, high, low], axis=1)
    right = jnp.concatenate([high, low, high], axis=1)
    return left, right


def whiten_kernel(z_ref, near_ref, far_ref, out_ref, core_ref, *, bits_c):
    relations, halves = out_ref.shape[0], near_ref.shape[0]
    pieces = 2 * halves // relations
    my_col = lax.axis_index("cols")
    my_row = lax.axis_index("rows")
    left, right = whiten_parts(z_ref)
    core_ref[:halves] = near_ref[...]
    core_ref[halves:] = far_ref[...]
    for k in range(relations):
        parts = []
        for p in range(pieces):
            place = reversed_slot((k * pieces + p) ^ my_col, bits_c)
            parts += [unpacked_block(core_ref[place, h ^ (my_row & 1)]) for h in range(2)]
        core = jnp.concatenate(parts, axis=0)
        out_ref[k] = whitened(left, right, core)


def half_whiten_kernel(z_ref, core_ref, *refs, bits_c):
    out_ref = refs[-1]
    my_col = lax.axis_index("cols")
    my_row = lax.axis_index("rows")
    left, right = whiten_parts(z_ref)
    for p in range(core_ref.shape[0]):
        slot = 2 * reversed_slot(p, bits_c - 1)
        parts = [unpacked_block(core_ref[p, h ^ (my_row & 1)]) for h in range(2)]
        core = jnp.concatenate(parts, axis=0)
        result = whitened(left, right, core)
        if len(refs) == 1:
            out_ref[p] = result
        else:
            out_ref[slot ^ my_col] = refs[0][p]
            out_ref[(slot + 1) ^ my_col] = result


def whiten(z, near, far, relations):
    rank = z.shape[0]
    halves = near.shape[0]
    vmem = pl.BlockSpec(memory_space=pltpu.VMEM)

    def call(kernel, count, microseconds, *args, scratch=()):
        return pl.pallas_call(
            functools.partial(kernel, bits_c=bits_of("cols")),
            out_shape=jax.ShapeDtypeStruct((count, rank, rank), jnp.float32),
            in_specs=[vmem] * (1 + len(args)),
            out_specs=vmem,
            scratch_shapes=scratch,
            compiler_params=params(),
            cost_estimate=cost(microseconds),
            name="whiten",
        )(z, *args)

    if 2 * halves != relations:
        scratch = [pltpu.VMEM((2 * halves,) + near.shape[1:], jnp.float32)]
        return call(whiten_kernel, relations, 2.3, near, far, scratch=scratch)
    first = call(half_whiten_kernel, halves, 1.2, near)
    return call(half_whiten_kernel, relations, 1.2, far, first)


def pair_of_sums(x):
    for b in range(bits_of("cols") - 1):
        x = x + swap(x, "cols", 1 << b)
    return x, swap(x, "cols", 1 << (bits_of("cols") - 1))


def local(factor, cores, tile_values, tile_rows, tile_cols, tile_counts):
    relations, slots, tile, _ = tile_values.shape
    rank = factor.shape[1]
    n_rows, n_cols = lax.axis_size("rows"), lax.axis_size("cols")
    half = n_rows // 2
    places, scale, tiles, cores, own = prepare(
        tile_rows, tile_cols, tile_counts, tile_values, cores, factor
    )

    factors, gram = gram_of([own] + gather_rows(factor, own)[1:])
    panel = gather_cols(factor)
    gram_pair = pair_of_sums(gram)
    direct, back = first_pass(places, scale, tiles, after(factors, gram_pair[0]), panel, cores)
    direct, back = after((direct, back), gram_pair)
    system = square_call(system_kernel, "system", 3.8, rank, *gram_pair, cores)
    middle = half + half // 2
    far = swap(back[middle:].astype(jnp.float16), "rows", 1).astype(jnp.float32)
    close = swap(back[half:middle].astype(jnp.float16), "rows", 1).astype(jnp.float32)
    far = back[half // 2:half] + far
    close = back[:half // 2] + close
    packed = [
        after(x[i].astype(jnp.float16), system) for x in (close, far) for i in range(half // 2)
    ]
    packed[half - 1] = after(packed[half - 1], close)
    received = [swap(packed[i], "rows", 2 * i).astype(jnp.float32) for i in range(1, half)]
    numerator = scatter_cols(direct)[0] + close[0] + functools.reduce(jnp.add, received)
    inverse = square_call(inverse_kernel, "inverse", 5.2, rank, system, scale, scratch=True)
    factor_new = dot(numerator, inverse, precision=lax.Precision.HIGHEST).astype(jnp.bfloat16)

    factors_new, gram_new = gram_of(gather_rows(factor_new))
    panel_new = gather_cols(factor_new)
    gram_pair = pair_of_sums(gram_new)
    core = second_pass(places, tiles, factors_new, panel_new)
    keep, give = jnp.split(after(core, gram_pair[0]), 2, axis=0)
    bits = bits_of("cols")
    slots_left = [2 * reversed_slot(p, bits - 1) for p in range(n_cols // 2)]
    plane = [(h, p) for p in range(n_cols // 2) for h in range(2) if (h, p) != (0, 0)]
    core, packed = pack_plane(keep, swap(give, "cols", 1))
    packed = packed.astype(jnp.float16)
    core = merge(
        [core],
        [swap_both(packed[i], h, slots_left[p]) for i, (h, p) in enumerate(plane)],
    )
    z = square_call(begin_kernel, "begin", 3.3, rank, *gram_pair)
    core = merge([], [core] + [swap(core, "rows", 2 * i) for i in range(1, half)])
    core = after(core, z)
    found = {(h, p): swap_both(core, h, slots_left[p]) for h, p in plane}
    z = square_call(end_kernel, "end", 2.9, rank, after(z, found[plane[0]]))
    found[(0, 0)] = core
    near = jnp.stack(
        [jnp.stack([found[(h, p)] for h in range(2)]) for p in range(n_cols // 2)]
    )
    near = after(near, z)
    far = swap(near, "cols", 1)
    cores_new = whiten(z, near.astype(jnp.float32), far.astype(jnp.float32), relations)
    return (factor_new, cores_new)


def solution(mesh):
    in_specs = (
        P(("rows", "cols"), None),
        P(),
        P(None, "rows", "cols", None),
        P(None, "rows", "cols"),
        P(None, "rows", "cols"),
        P(None, "rows", "cols"),
    )
    out_specs = (P(("rows", "cols"), None), P())
    return jax.shard_map(local, mesh=mesh, in_specs=in_specs, out_specs=out_specs, check_vma=False)
```

```python
import functools

import jax
import jax.numpy as jnp
from jax import lax
from jax.experimental import pallas as pl
from jax.experimental.pallas import tpu as pltpu
from jax.sharding import PartitionSpec as P

ridge_weight = 0.1
product_bound = 672.0
f16_top = 30000.0
extra_rows = 16


def params():
    return pltpu.CompilerParams(vmem_limit_bytes=48 * 1024 * 1024)


def swap(x, axis, mask):
    size = lax.axis_size(axis)
    return lax.ppermute(x, axis, [(i, i ^ mask) for i in range(size)])


def swap_both(x, row_mask, col_mask):
    if col_mask == 0:
        return swap(x, "rows", row_mask)
    if row_mask == 0:
        return swap(x, "cols", col_mask)
    n_cols = lax.axis_size("cols")
    mask = row_mask * n_cols + col_mask
    size = lax.axis_size("rows") * n_cols
    return lax.ppermute(x, ("rows", "cols"), [(i, i ^ mask) for i in range(size)])


def cost(microseconds):
    return pl.CostEstimate(
        flops=int(microseconds * 1.1e9), bytes_accessed=100_000, transcendentals=0
    )


def after(x, other):
    return lax.optimization_barrier((x, other))[0]


def bits_of(axis):
    return lax.axis_size(axis).bit_length() - 1


def reversed_slot(slot, bits):
    out = 0
    for b in range(bits):
        out = out + (((slot >> b) & 1) << (bits - 1 - b))
    return out


def gather_cols(x):
    for b in range(bits_of("cols")):
        x = jnp.concatenate([x, swap(x, "cols", 1 << b)], axis=0)
    return x


def gather_rows(x, first=None):
    half = lax.axis_size("rows") // 2
    even = [swap(x, "rows", 2 * i) for i in range(1, half)]
    across = swap(x, "rows", 1)
    if first is not None:
        even = after(even, first)
    return [x] + even + [across] + [swap(p, "rows", 1) for p in even]


def tree_sum(parts):
    while len(parts) > 1:
        parts = [parts[i] + parts[i + 1] for i in range(0, len(parts), 2)]
    return parts[0]


def scatter_cols(x):
    for b in range(bits_of("cols")):
        keep, give = jnp.split(x, 2, axis=0)
        if b == 0:
            x = keep + swap(give, "cols", 1)
        else:
            x = keep + swap(give.astype(jnp.float16), "cols", 1 << b).astype(jnp.float32)
    return x


def dot(a, b, dims=((1,), (0,)), precision=None):
    return lax.dot_general(
        a, b, (dims, ((), ())), preferred_element_type=jnp.float32, precision=precision
    )


def gram_kernel(*refs):
    pieces, factors_ref, gram_ref = refs[:-2], refs[-2], refs[-1]
    begin = 0
    for piece in pieces:
        factors_ref[begin:begin + piece.shape[0], :] = piece[...]
        begin += piece.shape[0]
    whole = factors_ref[...]
    gram = dot(whole, whole, ((0,), (0,)))
    side = gram_ref.shape[1]
    gram_ref[0] = gram[:side, :side]
    gram_ref[1] = gram[:side, side:]
    gram_ref[2] = gram[side:, side:]


def gram_of(pieces):
    rank = pieces[0].shape[1]
    height = sum(piece.shape[0] for piece in pieces)
    vmem = pl.BlockSpec(memory_space=pltpu.VMEM)
    factors, gram = pl.pallas_call(
        gram_kernel,
        out_shape=(
            jax.ShapeDtypeStruct((height, rank), jnp.bfloat16),
            jax.ShapeDtypeStruct((3, rank // 2, rank // 2), jnp.float32),
        ),
        in_specs=[vmem] * len(pieces),
        out_specs=(vmem, vmem),
        compiler_params=params(),
        cost_estimate=cost(0.4),
        name="gram",
    )(*pieces)
    return factors, gram


def prepare_kernel(rows_hbm, cols_hbm, counts_ref, tiles_hbm, cores_hbm, factor_hbm,
                   places_ref, scale_ref, tiles_ref, copied_ref, own_ref,
                   rows_ref, cols_ref, sems, *, half, terms):
    relations, slots = tiles_ref.shape[0], tiles_ref.shape[1]
    my_row = lax.axis_index("rows")
    my_col = lax.axis_index("cols")
    copies = [
        pltpu.make_async_copy(source, target, sems.at[i])
        for i, (source, target) in enumerate(
            (
                (cores_hbm, copied_ref),
                (rows_hbm, rows_ref),
                (cols_hbm, cols_ref),
                (tiles_hbm, tiles_ref),
                (factor_hbm, own_ref),
            )
        )
    ]
    for copy in copies:
        copy.start()
    copies[0].wait()
    reach = jnp.zeros((1, 1), jnp.float32)
    for k in range(relations):
        size = jnp.abs(copied_ref[k].astype(jnp.float32))
        for axis in (0, 1):
            sums = jnp.sum(size, axis=axis, keepdims=True)
            reach = jnp.maximum(reach, jnp.max(sums, axis=1 - axis, keepdims=True))
    scale_ref[...] = jnp.broadcast_to(
        f16_top / (terms * relations * slots * product_bound * reach + 1e-20), scale_ref.shape
    )
    for copy in copies[1:]:
        copy.wait()
    for k in range(relations):
        for s in range(slots):
            col = cols_ref[k, 0, s] ^ my_row
            places_ref[k, s] = (col & 1) * half + (col >> 1)
            places_ref[k, slots + s] = rows_ref[k, 0, s] ^ my_col

            @pl.when(s >= counts_ref[k, 0, 0])
            def _():
                tiles_ref[k, s] = jnp.zeros(tiles_ref.shape[2:], tiles_ref.dtype)


def stay(x):
    return pltpu.with_memory_space_constraint(x, pltpu.HBM)


def prepare(rows, cols, counts, tiles, cores, factor):
    n_rows, n_cols = lax.axis_size("rows"), lax.axis_size("cols")
    smem = pl.BlockSpec(memory_space=pltpu.SMEM)
    vmem = pl.BlockSpec(memory_space=pltpu.VMEM)
    anywhere = pl.BlockSpec(memory_space=pltpu.HBM)
    return pl.pallas_call(
        functools.partial(prepare_kernel, half=n_rows // 2, terms=2.0 * n_cols),
        out_shape=(
            jax.ShapeDtypeStruct((tiles.shape[0], 2 * tiles.shape[1]), jnp.int32),
            jax.ShapeDtypeStruct((1, cores.shape[-1]), jnp.float32),
            jax.ShapeDtypeStruct(tiles.shape, tiles.dtype),
            jax.ShapeDtypeStruct(cores.shape, cores.dtype),
            jax.ShapeDtypeStruct(factor.shape, factor.dtype),
        ),
        in_specs=[anywhere, anywhere, smem, anywhere, anywhere, anywhere],
        out_specs=(smem, vmem, vmem, vmem, vmem),
        scratch_shapes=[
            pltpu.SMEM(rows.shape, jnp.int32),
            pltpu.SMEM(cols.shape, jnp.int32),
            pltpu.SemaphoreType.DMA((5,)),
        ],
        compiler_params=params(),
        cost_estimate=cost(2.0),
        name="prepare",
    )(
        stay(rows), stay(cols), counts, stay(tiles), stay(cores), stay(factor)
    )


def first_kernel(places_ref, scale_ref, tiles_ref, factors_ref, panel_ref, cores_ref,
                 direct_ref, back_ref, acc_ref, turned_ref, sums_ref, *, bits_c):
    relations, slots = tiles_ref.shape[0], tiles_ref.shape[1]
    tile = tiles_ref.shape[2]
    panels = panel_ref.shape[0] // tile
    sums_ref[...] = jnp.zeros_like(sums_ref)
    for k in range(relations):
        core = cores_ref[k]
        for i in range(panels):
            rotated = dot(panel_ref[i * tile:(i + 1) * tile, :], core).astype(jnp.bfloat16)
            turned_ref[i] = rotated.T
        acc_ref[...] = jnp.zeros_like(acc_ref)
        for s in range(slots):
            values = tiles_ref[k, s]
            col = places_ref[k, s]
            row = places_ref[k, slots + s]
            acc_ref[row] += dot(values, factors_ref[col])
            sums_ref[col] += dot(turned_ref[row], values)
        for i in range(panels):
            whole = acc_ref[i]
            high = whole.astype(jnp.bfloat16)
            low = (whole - high.astype(jnp.float32)).astype(jnp.bfloat16)
            part = dot(high, core, ((1,), (1,))) + dot(low, core, ((1,), (1,)))
            part = part * scale_ref[...]
            place = reversed_slot(i, bits_c)
            if k == 0:
                direct_ref[place] = part
            else:
                direct_ref[place] += part
    for g in range(sums_ref.shape[0]):
        back_ref[g] = sums_ref[g].T * scale_ref[...]


def first_pass(places, scale, tiles, factors, panel, cores):
    tile = tiles.shape[2]
    rank = cores.shape[-1]
    n_rows, n_cols = lax.axis_size("rows"), lax.axis_size("cols")
    smem = pl.BlockSpec(memory_space=pltpu.SMEM)
    vmem = pl.BlockSpec(memory_space=pltpu.VMEM)
    return pl.pallas_call(
        functools.partial(first_kernel, bits_c=bits_of("cols")),
        out_shape=(
            jax.ShapeDtypeStruct((n_cols, tile, rank), jnp.float32),
            jax.ShapeDtypeStruct((n_rows, tile, rank), jnp.float32),
        ),
        in_specs=[smem, vmem, vmem, vmem, vmem, vmem],
        out_specs=(vmem, vmem),
        scratch_shapes=[
            pltpu.VMEM((n_cols, tile, rank), jnp.float32),
            pltpu.VMEM((n_cols, rank, tile), jnp.bfloat16),
            pltpu.VMEM((n_rows, rank, tile), jnp.float32),
        ],
        compiler_params=params(),
        cost_estimate=cost(4.8),
        name="first_pass",
    )(places, scale, tiles, factors.reshape(n_rows, tile, rank), panel, cores)


def second_kernel(places_ref, tiles_ref, factors_ref, panel_ref,
                  out_ref, turned_ref, upper_ref, picked_ref, *, bits_c):
    relations, slots = tiles_ref.shape[0], tiles_ref.shape[1]
    tile = tiles_ref.shape[2]
    panels = panel_ref.shape[0] // tile
    pieces = out_ref.shape[0] // relations
    height = out_ref.shape[2]
    my_row = lax.axis_index("rows")
    my_col = lax.axis_index("cols")
    for i in range(panels):
        turned_ref[i] = panel_ref[i * tile:(i + 1) * tile, :].T
    for k in range(relations):
        for s in range(slots):
            values = tiles_ref[k, s]
            col = places_ref[k, s]
            row = places_ref[k, slots + s]
            upper_ref[:, s * tile:(s + 1) * tile] = dot(turned_ref[row], values).astype(jnp.bfloat16)
            picked_ref[s * tile:(s + 1) * tile, :] = factors_ref[col]
        core = dot(upper_ref[...], picked_ref[...])
        for p in range(pieces):
            place = reversed_slot((k * pieces + p) ^ my_col, bits_c)
            for h in range(2):
                begin = (2 * p + h) * height
                out_ref[place, h ^ (my_row & 1)] = core[begin:begin + height, :]


def second_pass(places, tiles, factors, panel):
    relations, slots, tile, _ = tiles.shape
    rank = panel.shape[-1]
    n_rows, n_cols = lax.axis_size("rows"), lax.axis_size("cols")
    smem = pl.BlockSpec(memory_space=pltpu.SMEM)
    vmem = pl.BlockSpec(memory_space=pltpu.VMEM)
    return pl.pallas_call(
        functools.partial(second_kernel, bits_c=bits_of("cols")),
        out_shape=jax.ShapeDtypeStruct(
            (n_cols, 2, relations * rank // n_cols // 2, rank), jnp.float32
        ),
        in_specs=[smem, vmem, vmem, vmem],
        out_specs=vmem,
        scratch_shapes=[
            pltpu.VMEM((n_cols, rank, tile), jnp.bfloat16),
            pltpu.VMEM((rank, slots * tile), jnp.bfloat16),
            pltpu.VMEM((slots * tile, rank), jnp.bfloat16),
        ],
        compiler_params=params(),
        cost_estimate=cost(2.8),
        name="second_pass",
    )(places, tiles, factors.reshape(n_rows, tile, rank), panel)


def split(x, terms):
    parts = []
    for _ in range(terms):
        part = x.astype(jnp.bfloat16)
        parts.append(part)
        x = x - part.astype(jnp.float32)
    return parts


def eliminate(z_ref, begin, end, block, sub):
    size = z_ref.shape[0]
    wide = size // 128
    groups = block // 8
    rows = lax.broadcasted_iota(jnp.int32, (8, 128), 0)
    rows_wide = lax.broadcasted_iota(jnp.int32, (8, size), 0)
    lanes = lax.broadcasted_iota(jnp.int32, (8, size), 1)
    for p in range(begin, end):
        o = p * block
        panel = [z_ref[o + 8 * g:o + 8 * g + 8, :] for g in range(groups)]
        for q in range(block // sub):
            first = o + q * sub
            start = q * sub // 8
            cols = [
                {
                    g: jnp.broadcast_to(panel[g][:, first + m:first + m + 1], (8, 128))
                    for g in range(start, groups)
                }
                for m in range(sub)
            ]
            for m in range(sub):
                j = q * sub + m
                own, i = j // 8, j % 8
                root = lax.rsqrt(cols[m][own][i:i + 1, :])
                factors = {g: cols[m][g] * root for g in range(own, groups)}
                factors[own] = jnp.where(rows > i, factors[own], 0.0)
                for t in range(m + 1, sub):
                    line = cols[t][own][i:i + 1, :] * root
                    for g in range(own, groups):
                        cols[t][g] = cols[t][g] - factors[g] * line
                pivot = lanes == o + j
                panel[own] = jnp.where(pivot, jnp.where(rows_wide == i, 1.0, 0.0), panel[own])
                line = panel[own][i:i + 1, :] * jnp.concatenate([root] * wide, axis=1)
                for g in range(own, groups):
                    factor = jnp.concatenate([factors[g]] * wide, axis=1)
                    if g > own:
                        panel[g] = jnp.where(pivot, 0.0, panel[g])
                    panel[g] = panel[g] - factor * line
                panel[own] = jnp.where(rows_wide == i, line, panel[own])
        panel = jnp.concatenate(panel, axis=0)
        below = lax.broadcasted_iota(jnp.int32, (block, size), 0) + o
        across = lax.broadcasted_iota(jnp.int32, (block, size), 1)
        panel = jnp.where((across > below) & (across < o + block), 0.0, panel)
        z_ref[o:o + block, :] = panel
        rest = size - o - block
        if rest:
            high, mid, low = split(panel, 3)
            left = jnp.concatenate([high, high, mid, mid, high, low], axis=0)[:, o + block:]
            right = jnp.concatenate([high, mid, high, mid, low, high], axis=0)
            change = dot(left, right, ((0,), (0,)))
            spread = lax.broadcasted_iota(jnp.int32, (rest, size), 1)
            done = (spread >= o) & (spread < o + block)
            z_ref[o + block:, :] = jnp.where(done, 0.0, z_ref[o + block:, :]) - change


def lower_of(z):
    rows = lax.broadcasted_iota(jnp.int32, z.shape, 0)
    lanes = lax.broadcasted_iota(jnp.int32, z.shape, 1)
    return jnp.where(rows >= lanes, z, 0.0)


def system_kernel(mine_ref, other_ref, cores_ref, z_ref):
    size = z_ref.shape[0]
    side = size // 2
    upper = mine_ref[1] + other_ref[1]
    z_ref[:side, :side] = mine_ref[0] + other_ref[0]
    z_ref[:side, side:] = upper
    z_ref[side:, :side] = upper.T
    z_ref[side:, side:] = mine_ref[2] + other_ref[2]
    grams = jnp.concatenate(split(z_ref[...], 3), axis=0)
    rows = lax.broadcasted_iota(jnp.int32, (size, size), 0)
    lanes = lax.broadcasted_iota(jnp.int32, (size, size), 1)
    total = jnp.where(rows == lanes, ridge_weight, 0.0)
    for k in range(cores_ref.shape[0]):
        core = cores_ref[k]
        turned = core.T
        for left, right in ((core, turned), (turned, core)):
            middle = dot(jnp.concatenate([left] * 3, axis=1), grams)
            middle = jnp.concatenate(split(middle, 3), axis=1)
            total = total + dot(middle, jnp.concatenate([right] * 3, axis=0))
    z_ref[...] = total
    eliminate(z_ref, 0, size // 64, 32, 16)


def inverse_kernel(in_ref, scale_ref, out_ref, z_ref):
    size = z_ref.shape[0]
    z_ref[...] = in_ref[...]
    eliminate(z_ref, size // 64, size // 32, 32, 16)
    high, mid, low = split(lower_of(z_ref[...]), 3)
    left = jnp.concatenate([high, high, mid, mid, high, low], axis=0)
    right = jnp.concatenate([high, mid, high, mid, low, high], axis=0)
    out_ref[...] = dot(left, right, ((0,), (0,))) / scale_ref[...]


def power_of_two(exponent):
    left = jnp.abs(exponent)
    result = jnp.ones_like(exponent)
    for b in reversed(range(7)):
        taken = left >= float(1 << b)
        step = jnp.where(exponent < 0.0, 0.5 ** (1 << b), 2.0 ** (1 << b))
        result = jnp.where(taken, result * step, result)
        left = jnp.where(taken, left - float(1 << b), left)
    return result


def packed_block(x):
    top = jnp.maximum(jnp.max(jnp.abs(x), axis=0, keepdims=True), 1e-30)
    exponent = jnp.clip(jnp.ceil(jnp.log2(top)), -100.0, 126.0)
    exponents = jnp.broadcast_to(exponent, (extra_rows, x.shape[1]))
    return jnp.concatenate([x * power_of_two(-exponent), exponents], axis=0)


def unpacked_block(x):
    height = x.shape[0] - extra_rows
    return x[:height] * power_of_two(x[height:height + 1])


def plane_kernel(keep_ref, other_ref, own_ref, packed_ref):
    own_ref[...] = keep_ref[0, 0] + other_ref[0, 0]
    for i in range(packed_ref.shape[0]):
        p, h = (i + 1) // 2, (i + 1) % 2
        packed_ref[i] = packed_block(keep_ref[p, h] + other_ref[p, h])


def pack_plane(keep, other):
    pieces, _, height, rank = keep.shape
    vmem = pl.BlockSpec(memory_space=pltpu.VMEM)
    return pl.pallas_call(
        plane_kernel,
        out_shape=(
            jax.ShapeDtypeStruct((height, rank), jnp.float32),
            jax.ShapeDtypeStruct((2 * pieces - 1, height + extra_rows, rank), jnp.float32),
        ),
        in_specs=[vmem, vmem],
        out_specs=(vmem, vmem),
        compiler_params=params(),
        cost_estimate=cost(0.6),
        name="pack_plane",
    )(keep, other)


def merge_kernel(*refs, plain):
    parts = [ref[...] for ref in refs[:plain]]
    parts += [unpacked_block(ref[...]) for ref in refs[plain:-1]]
    refs[-1][...] = packed_block(tree_sum(parts))


def merge(plain, packed):
    args = list(plain) + [x.astype(jnp.float32) for x in packed]
    vmem = pl.BlockSpec(memory_space=pltpu.VMEM)
    merged = pl.pallas_call(
        functools.partial(merge_kernel, plain=len(plain)),
        out_shape=jax.ShapeDtypeStruct(args[-1].shape, jnp.float32),
        in_specs=[vmem] * len(args),
        out_specs=vmem,
        compiler_params=params(),
        cost_estimate=cost(0.5),
        name="merge",
    )(*args)
    return lax.optimization_barrier(merged.astype(jnp.float16))


def begin_kernel(mine_ref, other_ref, out_ref):
    size = out_ref.shape[0]
    side = size // 2
    out_ref[:side, :side] = mine_ref[0] + other_ref[0]
    out_ref[:side, side:] = mine_ref[1] + other_ref[1]
    out_ref[side:, :side] = jnp.zeros((side, side), jnp.float32)
    out_ref[side:, side:] = mine_ref[2] + other_ref[2]
    eliminate(out_ref, 0, size // 64, 32, 16)


def end_kernel(in_ref, out_ref):
    size = out_ref.shape[0]
    out_ref[...] = in_ref[...]
    eliminate(out_ref, size // 64, size // 32, 32, 16)


def square_call(kernel, name, microseconds, rank, *args, scratch=False):
    vmem = pl.BlockSpec(memory_space=pltpu.VMEM)
    return pl.pallas_call(
        kernel,
        out_shape=jax.ShapeDtypeStruct((rank, rank), jnp.float32),
        in_specs=[vmem] * len(args),
        out_specs=vmem,
        scratch_shapes=[pltpu.VMEM((rank, rank), jnp.float32)] if scratch else [],
        compiler_params=params(),
        cost_estimate=cost(microseconds),
        name=name,
    )(*args)


def whitened(left, right, core):
    first, rest = split(core, 2)
    middle = dot(left, jnp.concatenate([first, rest, first], axis=0))
    first, rest = split(middle, 2)
    return dot(jnp.concatenate([first, first, rest], axis=1), right, ((1,), (1,)))


def whiten_parts(z_ref):
    high, low = split(lower_of(z_ref[...]), 2)
    left = jnp.concatenate([high, high, low], axis=1)
    right = jnp.concatenate([high, low, high], axis=1)
    return left, right


def whiten_kernel(z_ref, near_ref, far_ref, out_ref, core_ref, *, bits_c):
    relations, halves = out_ref.shape[0], near_ref.shape[0]
    pieces = 2 * halves // relations
    my_col = lax.axis_index("cols")
    my_row = lax.axis_index("rows")
    left, right = whiten_parts(z_ref)
    core_ref[:halves] = near_ref[...]
    core_ref[halves:] = far_ref[...]
    for k in range(relations):
        parts = []
        for p in range(pieces):
            place = reversed_slot((k * pieces + p) ^ my_col, bits_c)
            parts += [unpacked_block(core_ref[place, h ^ (my_row & 1)]) for h in range(2)]
        core = jnp.concatenate(parts, axis=0)
        out_ref[k] = whitened(left, right, core)


def half_whiten_kernel(z_ref, core_ref, *refs, bits_c):
    out_ref = refs[-1]
    my_col = lax.axis_index("cols")
    my_row = lax.axis_index("rows")
    left, right = whiten_parts(z_ref)
    for p in range(core_ref.shape[0]):
        slot = 2 * reversed_slot(p, bits_c - 1)
        parts = [unpacked_block(core_ref[p, h ^ (my_row & 1)]) for h in range(2)]
        core = jnp.concatenate(parts, axis=0)
        result = whitened(left, right, core)
        if len(refs) == 1:
            out_ref[p] = result
        else:
            out_ref[slot ^ my_col] = refs[0][p]
            out_ref[(slot + 1) ^ my_col] = result


def whiten(z, near, far, relations):
    rank = z.shape[0]
    halves = near.shape[0]
    vmem = pl.BlockSpec(memory_space=pltpu.VMEM)

    def call(kernel, count, microseconds, *args, scratch=()):
        return pl.pallas_call(
            functools.partial(kernel, bits_c=bits_of("cols")),
            out_shape=jax.ShapeDtypeStruct((count, rank, rank), jnp.float32),
            in_specs=[vmem] * (1 + len(args)),
            out_specs=vmem,
            scratch_shapes=scratch,
            compiler_params=params(),
            cost_estimate=cost(microseconds),
            name="whiten",
        )(z, *args)

    if 2 * halves != relations:
        scratch = [pltpu.VMEM((2 * halves,) + near.shape[1:], jnp.float32)]
        return call(whiten_kernel, relations, 2.3, near, far, scratch=scratch)
    first = call(half_whiten_kernel, halves, 1.2, near)
    return call(half_whiten_kernel, relations, 1.2, far, first)


def pair_of_sums(x):
    for b in range(bits_of("cols") - 1):
        x = x + swap(x, "cols", 1 << b)
    return x, swap(x, "cols", 1 << (bits_of("cols") - 1))


def local(factor, cores, tile_values, tile_rows, tile_cols, tile_counts):
    relations, slots, tile, _ = tile_values.shape
    rank = factor.shape[1]
    n_rows, n_cols = lax.axis_size("rows"), lax.axis_size("cols")
    half = n_rows // 2
    places, scale, tiles, cores, own = prepare(
        tile_rows, tile_cols, tile_counts, tile_values, cores, factor
    )

    factors, gram = gram_of([own] + gather_rows(factor, own)[1:])
    panel = gather_cols(factor)
    gram_pair = pair_of_sums(gram)
    direct, back = first_pass(places, scale, tiles, after(factors, gram_pair[0]), panel, cores)
    direct, back = after((direct, back), gram_pair)
    system = square_call(system_kernel, "system", 3.8, rank, *gram_pair, cores)
    middle = half + half // 2
    far = swap(back[middle:].astype(jnp.float16), "rows", 1).astype(jnp.float32)
    close = swap(back[half:middle].astype(jnp.float16), "rows", 1).astype(jnp.float32)
    far = back[half // 2:half] + far
    close = back[:half // 2] + close
    packed = [
        after(x[i].astype(jnp.float16), system) for x in (close, far) for i in range(half // 2)
    ]
    packed[half - 1] = after(packed[half - 1], close)
    received = [swap(packed[i], "rows", 2 * i).astype(jnp.float32) for i in range(1, half)]
    numerator = scatter_cols(direct)[0] + close[0] + functools.reduce(jnp.add, received)
    inverse = square_call(inverse_kernel, "inverse", 5.2, rank, system, scale, scratch=True)
    factor_new = dot(numerator, inverse, precision=lax.Precision.HIGHEST).astype(jnp.bfloat16)

    factors_new, gram_new = gram_of(gather_rows(factor_new))
    panel_new = gather_cols(factor_new)
    gram_pair = pair_of_sums(gram_new)
    core = second_pass(places, tiles, factors_new, panel_new)
    keep, give = jnp.split(after(core, gram_pair[0]), 2, axis=0)
    bits = bits_of("cols")
    slots_left = [2 * reversed_slot(p, bits - 1) for p in range(n_cols // 2)]
    plane = [(h, p) for p in range(n_cols // 2) for h in range(2) if (h, p) != (0, 0)]
    core, packed = pack_plane(keep, swap(give, "cols", 1))
    packed = packed.astype(jnp.float16)
    core = merge(
        [core],
        [swap_both(packed[i], h, slots_left[p]) for i, (h, p) in enumerate(plane)],
    )
    z = square_call(begin_kernel, "begin", 3.3, rank, *gram_pair)
    core = merge([], [core] + [swap(core, "rows", 2 * i) for i in range(1, half)])
    core = after(core, z)
    found = {(h, p): swap_both(core, h, slots_left[p]) for h, p in plane}
    z = square_call(end_kernel, "end", 2.9, rank, after(z, found[plane[0]]))
    found[(0, 0)] = core
    near = jnp.stack(
        [jnp.stack([found[(h, p)] for h in range(2)]) for p in range(n_cols // 2)]
    )
    near = after(near, z)
    far = swap(near, "cols", 1)
    cores_new = whiten(z, near.astype(jnp.float32), far.astype(jnp.float32), relations)
    return (factor_new, cores_new)


def solution(mesh):
    in_specs = (
        P(("rows", "cols"), None),
        P(),
        P(None, "rows", "cols", None),
        P(None, "rows", "cols"),
        P(None, "rows", "cols"),
        P(None, "rows", "cols"),
    )
    out_specs = (P(("rows", "cols"), None), P())
    return jax.shard_map(local, mesh=mesh, in_specs=in_specs, out_specs=out_specs, check_vma=False)
```
